512 devices in a mesh: blk: 16 (over z, y_lo), tan: 32 (over y_hi, x, core).
Axes of the slice: x: 4, y: 8 (y_hi: 4, y_lo: 2; y = y_hi * 2 + y_lo), z: 8, core: 2. Of those that a mesh axis runs over, the one named last changes fastest.
Arguments:
- layer_in: bfloat16 [2048, 256], P('blk'), may hold values from -6 to 6
- laplace_in: bfloat16 [2048, 256], P('blk'), may hold values from -6 to 6
- tangent_in: bfloat16 [2048, 64, 256], P('blk', 'tan'), may hold values from -1.5 to 1.5
- spin_labels: int32 [2048], P('blk'), may hold values from 0 to 1
- pair_bias: bfloat16 [2048, 2048], P('blk'), may hold values from -6 to 306
- query_weight: bfloat16 [256, 256], replicated, may hold values from -0.375 to 0.375
- key_weight: bfloat16 [256, 256], replicated, may hold values from -0.375 to 0.375
- value_weight: bfloat16 [256, 256], replicated, may hold values from -0.375 to 0.375
- out_weight: bfloat16 [256, 256], replicated, may hold values from -0.375 to 0.375
- head_gain: float32 [4], replicated, may hold values from 0.5 to 2
- spin_gain: float32 [4], replicated, may hold values from -2 to 2
Outputs:
- layer_out: bfloat16 [2048, 256], P('blk')
- tangent_out: bfloat16 [2048, 64, 256], P('blk', 'tan')
- laplacian_out: float32 [2048, 256], P('blk')
The draws below stay inside these ranges and needn't reach their ends.
All inputs are finite; a program needn't handle non-finite values.
Results may differ from the reference program's by a relative error of at most 0.02.
Values may be sent and summed in bfloat16 or wider, within the bound.
A program may use at most 64 MiB of HBM per device.

```python
import math
import jax
import jax.numpy as jnp
from jax import lax

D = 256
H = 4
NQ_DEV = 128
N = 2048
TANG = 64


def draw_pair_bias(key, part):
    base = jnp.clip(jax.random.normal(key, (N, N), jnp.float32), -6.0, 6.0)
    return base.astype(jnp.bfloat16)


def place_ends(values, rng, smallest, high):
    longest = values.shape.index(max(values.shape))
    spots = []
    for shift in (0, 1):
        where = [jax.random.randint(jax.random.fold_in(rng, axis), (), 0, length) for axis, length in enumerate(values.shape)]
        where[longest] = (where[longest] + shift) % values.shape[longest]
        spots.append(tuple(where))
    return values.at[spots[0]].set(smallest).at[spots[1]].set(high)


def block_scale(rng, dims, pieces, least, largest):
    def one(dim, blocks):
        draws = jax.random.uniform(jax.random.fold_in(jax.random.fold_in(rng, 6), dim), (blocks,), jnp.float32, least / len(pieces), largest / len(pieces))
        return jnp.repeat(jnp.exp(draws), dims[dim] // blocks).reshape((-1,) + (1,) * (len(dims) - dim - 1))

    level = one(*pieces[0])
    for cut in pieces[1:]:
        level = level * one(*cut)
    return level


def scatter_about(key, shape, scale, limit, cuts=(), held_as=jnp.bfloat16):
    array = jax.random.normal(key, shape, jnp.float32) * scale
    if len(cuts) > 0:
        array = block_scale(key, shape, cuts, -0.22, 0.18) * array
    return jnp.clip(array, min=-limit, max=limit).astype(held_as)


def setup_inputs(seed: int = 0) -> dict:
    key_list = jax.random.split(jax.random.key(seed), 12)
    layer_in = scatter_about(key_list[0], (N, D), 1.0, 6.0, ((0, 16),))
    laplace_in = scatter_about(key_list[1], (N, D), 1.0, 6.0, ((0, 16),))
    tangent_in = scatter_about(key_list[2], (N, TANG, D), 0.25, 1.5, ((0, 16), (1, 32)))
    spin_labels = place_ends(jax.random.randint(key_list[3], (N,), 0, 2), jax.random.fold_in(key_list[3], 1), 0, 1).astype(jnp.int32)
    pair_bias = draw_pair_bias(jax.random.fold_in(key_list[11], 71), 0)
    query_weight = scatter_about(key_list[5], (D, D), D ** -0.5, 0.375)
    key_weight = scatter_about(key_list[6], (D, D), D ** -0.5, 0.375)
    value_weight = scatter_about(key_list[7], (D, D), D ** -0.5, 0.375)
    out_weight = scatter_about(key_list[8], (D, D), D ** -0.5, 0.375)
    head_gain = jnp.clip(jax.random.uniform(key_list[9], (H,), jnp.float32, 0.5, 2.0), 0.5, 2.0)
    spin_gain = jnp.clip(jax.random.uniform(key_list[10], (H,), jnp.float32, -2.0, 2.0), -2.0, 2.0)
    return {"layer_in": layer_in, "laplace_in": laplace_in, "tangent_in": tangent_in, "spin_labels": spin_labels, "pair_bias": pair_bias, "query_weight": query_weight, "key_weight": key_weight, "value_weight": value_weight, "out_weight": out_weight, "head_gain": head_gain, "spin_gain": spin_gain}


def to_bfloat(values):
    return lax.optimization_barrier(values.astype(jnp.bfloat16)).astype(jnp.float32)

def project(rows, weight):
    return jnp.dot(rows, weight, preferred_element_type=jnp.float32).astype(jnp.bfloat16)

def reference(layer_in, laplace_in, tangent_in, spin_labels, pair_bias, query_weight, key_weight, value_weight, out_weight, head_gain, spin_gain):
    count, width = layer_in.shape
    heads = head_gain.shape[0]
    head_size = width // heads
    dirs = tangent_in.shape[1]
    scale = 1.0 / math.sqrt(head_size)
    flat_tan = tangent_in.reshape(count * dirs, width)
    queries = project(layer_in, query_weight)
    keys = project(layer_in, key_weight)
    values = project(layer_in, value_weight)
    lap_queries = project(laplace_in, query_weight)
    lap_keys = project(laplace_in, key_weight)
    lap_values = project(laplace_in, value_weight)
    tan_queries = project(flat_tan, query_weight).reshape(count, dirs, width)
    tan_keys = project(flat_tan, key_weight).reshape(count, dirs, width)
    tan_values = project(flat_tan, value_weight).reshape(count, dirs, width)
    key_h = keys.astype(jnp.float32).reshape(count, heads, head_size)
    value_h = values.astype(jnp.float32).reshape(count, heads, head_size)
    lap_key_h = lap_keys.astype(jnp.float32).reshape(count, heads, head_size)
    lap_value_h = lap_values.astype(jnp.float32).reshape(count, heads, head_size)
    tan_key_t = jnp.transpose(tan_keys, (1, 0, 2)).astype(jnp.float32).reshape(dirs, count, heads, head_size)
    tan_value_t = jnp.transpose(tan_values, (1, 0, 2)).astype(jnp.float32).reshape(dirs, count, heads, head_size)
    spin_all = spin_labels.astype(jnp.float32)
    blocks = count // NQ_DEV

    def one_block(index):
        first = (index * NQ_DEV).astype(jnp.int32)
        query_b = lax.dynamic_slice_in_dim(queries, first, NQ_DEV, 0).astype(jnp.float32).reshape(NQ_DEV, heads, head_size)
        lap_query_b = lax.dynamic_slice_in_dim(lap_queries, first, NQ_DEV, 0).astype(jnp.float32).reshape(NQ_DEV, heads, head_size)
        tan_query_b = lax.dynamic_slice_in_dim(tan_queries, first, NQ_DEV, 0).astype(jnp.float32).reshape(NQ_DEV, dirs, heads, head_size)
        tan_query_t = jnp.transpose(tan_query_b, (1, 0, 2, 3))
        bias_b = lax.dynamic_slice_in_dim(pair_bias, first, NQ_DEV, 1).astype(jnp.float32)
        spin_b = lax.dynamic_slice_in_dim(spin_all, first, NQ_DEV, 0)
        same = spin_b[:, None] * spin_all[None, :] + (1.0 - spin_b)[:, None] * (1.0 - spin_all)[None, :]
        scores = jnp.einsum('ihd,jhd->hij', query_b, key_h) * scale
        scores = scores + head_gain[:, None, None] * bias_b.T[None] + spin_gain[:, None, None] * same[None]
        top = lax.optimization_barrier(jnp.max(scores, axis=2, keepdims=True))
        unnorm = jnp.exp(scores - top)
        weights = to_bfloat(unnorm)
        total = lax.optimization_barrier(jnp.sum(unnorm, axis=2))
        numer = jnp.einsum('hij,jhd->ihd', weights, value_h)
        lap_scores = (jnp.einsum('ihd,jhd->hij', lap_query_b, key_h) + jnp.einsum('ihd,jhd->hij', query_b, lap_key_h)) * scale
        lap_weighted = unnorm * lap_scores
        lap_total = lax.optimization_barrier(jnp.sum(lap_weighted, axis=2))
        lap_numer = jnp.einsum('hij,jhd->ihd', to_bfloat(lap_weighted), value_h) + jnp.einsum('hij,jhd->ihd', weights, lap_value_h)

        def direction(carry, item):
            trace_total, trace_numer = carry
            tan_q, tan_k, tan_v = item
            tan_scores = (jnp.einsum('ihd,jhd->hij', tan_q, key_h) + jnp.einsum('ihd,jhd->hij', query_b, tan_k)) * scale
            cross = jnp.einsum('ihd,jhd->hij', tan_q, tan_k) * scale
            tan_weighted = unnorm * tan_scores
            tan_weights = to_bfloat(tan_weighted)
            tan_total = lax.optimization_barrier(jnp.sum(tan_weighted, axis=2))
            tan_numer = jnp.einsum('hij,jhd->ihd', tan_weights, value_h) + jnp.einsum('hij,jhd->ihd', weights, tan_v)
            second = unnorm * (tan_scores * tan_scores + 2.0 * cross)
            trace_total = trace_total + lax.optimization_barrier(jnp.sum(second, axis=2))
            trace_numer = trace_numer + jnp.einsum('hij,jhd->ihd', to_bfloat(second), value_h) + 2.0 * jnp.einsum('hij,jhd->ihd', tan_weights, tan_v)
            return ((trace_total, trace_numer), (tan_total, tan_numer))
        start_carry = (jnp.zeros((heads, NQ_DEV), jnp.float32), jnp.zeros((NQ_DEV, heads, head_size), jnp.float32))
        (trace_total, trace_numer), (tan_totals, tan_numers) = lax.scan(direction, start_carry, (tan_query_t, tan_key_t, tan_value_t))
        denom = total.T[:, :, None]
        attn = numer / denom
        tan_denom = jnp.transpose(tan_totals, (0, 2, 1))[..., None]
        attn_tan = tan_numers / denom[None] - numer[None] * tan_denom / (denom * denom)[None]
        cross_sum = lax.optimization_barrier(jnp.sum(tan_numers * tan_denom, axis=0))
        square_sum = lax.optimization_barrier(jnp.sum(tan_denom * tan_denom, axis=0))
        attn_lap = (lap_numer + trace_numer) / denom - numer * (lap_total.T[:, :, None] + trace_total.T[:, :, None]) / (denom * denom)
        attn_lap = attn_lap - 2.0 * cross_sum / (denom * denom) + 2.0 * numer * square_sum / (denom * denom * denom)
        layer_b = lax.dynamic_slice_in_dim(layer_in, first, NQ_DEV, 0)
        laplace_b = lax.dynamic_slice_in_dim(laplace_in, first, NQ_DEV, 0)
        tangent_b = lax.dynamic_slice_in_dim(tangent_in, first, NQ_DEV, 0)
        out_layer = (jnp.dot(attn.reshape(NQ_DEV, width).astype(jnp.bfloat16), out_weight, preferred_element_type=jnp.float32) + layer_b.astype(jnp.float32)).astype(jnp.bfloat16)
        tan_flat = jnp.transpose(attn_tan, (1, 0, 2, 3)).reshape(NQ_DEV * dirs, width).astype(jnp.bfloat16)
        out_tan = jnp.dot(tan_flat, out_weight, preferred_element_type=jnp.float32).reshape(NQ_DEV, dirs, width)
        out_tan = (out_tan + tangent_b.astype(jnp.float32)).astype(jnp.bfloat16)
        out_lap = jnp.dot(attn_lap.reshape(NQ_DEV, width).astype(jnp.bfloat16), out_weight, preferred_element_type=jnp.float32) + laplace_b.astype(jnp.float32)
        return (out_layer, out_tan, out_lap)
    out_layer, out_tan, out_lap = lax.map(one_block, jnp.arange(blocks, dtype=jnp.int32))
    return (out_layer.reshape(count, width), out_tan.reshape(count, dirs, width), out_lap.reshape(count, width))
```

```python
import functools

import jax
import jax.numpy as jnp
from jax import lax
from jax.experimental import pallas as pl
from jax.experimental.pallas import tpu as pltpu
from jax.sharding import PartitionSpec as P

MESH = pl.DeviceIdType.MESH
F32 = jnp.float32
BF16 = jnp.bfloat16
ROWS = 128
HALF = 64
WIDTH = 256
HEADS = 4
HEAD = 64
CORES = 2


def dot(a, b):
    return jnp.dot(a, b, preferred_element_type=F32)


def dot_t(a, b):
    return lax.dot_general(a, b, (((1,), (1,)), ((), ())), preferred_element_type=F32)


def kernel(
    nz,
    tans,
    layer_hbm,
    lap_hbm,
    tan_hbm,
    spin_hbm,
    bias_hbm,
    wq_hbm,
    wk_hbm,
    wv_hbm,
    wo_hbm,
    hg_ref,
    sg_ref,
    layer_out,
    tan_out,
    lap_out,
    wq,
    wk,
    wv,
    wo,
    wvt,
    lap_own,
    spin_own,
    g_l,
    g_t,
    g_r,
    g_b,
    g_s,
    g_x,
    qa,
    qb,
    qc,
    ql,
    kk,
    vt,
    s_bias,
    s_same,
    s_spin,
    top_ref,
    acc,
    sums,
    a_attn,
    a_tan,
    own,
    rs,
    red,
    ag,
    local_sem,
    t_z_send,
    t_z_recv,
    t_y_send,
    t_y_recv,
    l_z_send,
    l_z_recv,
    l_y_send,
    l_y_recv,
    l_c_send,
    l_c_recv,
    r_z_send,
    r_z_recv,
    r_y_send,
    r_y_recv,
    b_d_send,
    b_d_recv,
    b_c_send,
    b_c_recv,
    s_send,
    s_recv,
    x_send,
    x_recv,
    rs_send,
    rs_recv,
    ag_send,
    ag_recv,
):
    blk = lax.axis_index("blk")
    tan = lax.axis_index("tan")
    blks = 2 * nz
    z = blk // 2
    y = blk % 2
    core = tan % 2
    my_half = pl.ds(pl.multiple_of(core * HALF, HALF), HALF)

    barrier = pltpu.get_barrier_semaphore()

    def greet_blk(k, carry):
        pl.semaphore_signal(
            barrier, inc=1, device_id={"blk": (blk + k) % blks}, device_id_type=MESH
        )
        return carry

    def greet_tan(k, carry):
        pl.semaphore_signal(
            barrier, inc=1, device_id={"tan": (tan + k) % tans}, device_id_type=MESH
        )
        return carry

    lax.fori_loop(1, blks, greet_blk, 0)
    lax.fori_loop(1, tans, greet_tan, 0)

    own_cols = pl.ds(pl.multiple_of(blk * ROWS, ROWS), ROWS)
    local = [
        (tan_hbm.at[0], g_t.at[0, 0]),
        (layer_hbm, g_l.at[0, 0]),
        (tan_hbm.at[1], g_r.at[0, 0]),
        (wq_hbm, wq),
        (wk_hbm, wk),
        (wv_hbm, wv),
        (lap_hbm, lap_own),
        (spin_hbm, spin_own),
        (bias_hbm.at[:, own_cols], g_b.at[0, 0]),
        (wo_hbm, wo),
    ]
    local = [
        pltpu.make_async_copy(src, dst, local_sem.at[n]) for n, (src, dst) in enumerate(local)
    ]
    for copy in local:
        copy.start()

    up_z = {"blk": ((z + 1) % nz) * 2 + y}
    down_z = {"blk": ((z + nz - 1) % nz) * 2 + y}
    other_y = {"blk": z * 2 + (1 - y)}
    other_core = {"tan": tan + 1 - 2 * core}

    started = []

    def remote(src, dst, send, recv, device):
        return pltpu.make_async_remote_copy(
            src_ref=src,
            dst_ref=dst,
            send_sem=send,
            recv_sem=recv,
            device_id=device,
            device_id_type=MESH,
        )

    def before(o, up):
        return (o - 1, up_z) if up else ((o + 1) % nz, down_z)

    last_up = nz // 2
    last_up_r = nz - 1 - last_up

    def flow_t(o):
        src, device = before(o, o <= last_up)
        return remote(g_t.at[src, 0], g_t.at[o, 0], t_z_send.at[o], t_z_recv.at[o], device)

    def flow_l(o):
        src, device = before(o, o <= last_up)
        return remote(
            g_l.at[src, 0, my_half],
            g_l.at[o, 0, my_half],
            l_z_send.at[o],
            l_z_recv.at[o],
            device,
        )

    def flow_r(o, side):
        src, device = before(o, o <= last_up_r)
        return remote(
            g_r.at[src, side],
            g_r.at[o, side],
            r_z_send.at[o, side],
            r_z_recv.at[o, side],
            device,
        )

    def cross_t(o):
        return remote(g_t.at[o, 0], g_t.at[o, 1], t_y_send.at[o], t_y_recv.at[o], other_y)

    def cross_l(o):
        return remote(
            g_l.at[o, 0, my_half],
            g_l.at[o, 1, my_half],
            l_y_send.at[o],
            l_y_recv.at[o],
            other_y,
        )

    cross_r = remote(g_r.at[0, 0], g_r.at[0, 1], r_y_send.at[0], r_y_recv.at[0], other_y)

    def mate_l(o, side):
        return remote(
            g_l.at[o, side, my_half],
            g_l.at[o, side, my_half],
            l_c_send.at[o, side],
            l_c_recv.at[o, side],
            other_core,
        )

    def mate_b(o, side):
        return remote(
            g_b.at[o, side, my_half],
            g_b.at[o, side, my_half],
            b_c_send.at[o, side],
            b_c_recv.at[o, side],
            other_core,
        )

    def peer(o, side):
        return ((z + o) % nz) * 2 + (y + side) % 2

    def direct_b(o, side):
        there = peer(o, side)
        columns = pl.ds(pl.multiple_of(there * ROWS, ROWS), ROWS)
        return remote(
            bias_hbm.at[my_half, columns],
            g_b.at[o, side, my_half],
            b_d_send.at[o, side],
            b_d_recv.at[o, side],
            {"blk": there},
        )

    def direct_s(o, side):
        return remote(
            spin_hbm,
            g_s.at[o, side],
            s_send.at[o, side],
            s_recv.at[o, side],
            {"blk": peer(o, side)},
        )

    def start(copy):
        copy.start()
        started.append(copy)

    def next_of(o, last):
        if o == 0:
            return [n for n in (1, nz - 1) if n in arrivals(1, last)]
        if o <= last:
            return [o + 1] if o < last else []
        return [o - 1] if o - 1 > last else []

    def arrivals(step, last):
        found = [step] if step <= last else []
        down = nz - step
        if down > last and down != step or (down == step and step > last):
            found.append(down)
        return found

    share_o = tan // 4
    share_y = (tan // 2) % 2
    is_own = tan < 2
    share_to = ((z + share_o) % nz) * 2 + (y + share_y) % 2
    copy_x = remote(lap_hbm.at[my_half], g_x, x_send.at[0], x_recv.at[0], {"blk": share_to})
    copy_x_own = pltpu.make_async_copy(lap_hbm.at[my_half], g_x, local_sem.at[10])

    for copy in local[:3]:
        copy.wait()
    pl.semaphore_wait(barrier, blks - 1 + tans - 1)

    for o in next_of(0, last_up):
        start(flow_t(o))
    start(cross_t(0))
    for o in next_of(0, last_up):
        start(flow_l(o))
    start(cross_r)
    start(cross_l(0))
    for o in next_of(0, last_up_r):
        start(flow_r(o, 0))
    order = [0]
    for step in range(1, nz // 2 + 1):
        order += sorted({step, nz - step})
    for o in order:
        for side in (0, 1):
            if (o, side) != (0, 0):
                start(direct_s(o, side))
                start(direct_b(o, side))

    @pl.when(is_own)
    def _():
        copy_x_own.start()

    @pl.when(jnp.logical_not(is_own))
    def _():
        copy_x.start()

    for copy in local[3:]:
        copy.wait()

    wvt[...] = jnp.transpose(wv[...].astype(F32)).astype(BF16)
    lanes = lax.broadcasted_iota(jnp.int32, (ROWS, ROWS), 1)

    def queries(rows):
        return dot(rows, wq[...]).astype(BF16).astype(F32) * 0.125

    q = queries(g_l[0, 0])
    q0 = queries(g_t[0, 0])
    q1 = queries(g_r[0, 0])
    qlap = queries(lap_own[...])
    for pair in range(2):
        cols = slice(pair * ROWS, (pair + 1) * ROWS)
        for e in range(2):
            keep = (lanes >= e * HEAD) & (lanes < (e + 1) * HEAD)

            def part(value, scale=1.0):
                return jnp.where(keep, value[:, cols] * scale, 0.0).astype(BF16)

            first = slice(e * ROWS, (e + 1) * ROWS)
            second = slice((2 + e) * ROWS, (3 + e) * ROWS)
            left, right = slice(0, ROWS), slice(ROWS, 2 * ROWS)
            zero = jnp.zeros((ROWS, ROWS), BF16)
            qa[pair, first, left] = part(q)
            qa[pair, first, right] = zero
            qa[pair, second, left] = part(q0)
            qa[pair, second, right] = part(q)
            qb[pair, first, left] = part(q1)
            qb[pair, first, right] = part(q)
            qc[pair, first, left] = part(q0, 2.0)
            qc[pair, first, right] = part(q1, 2.0)
            ql[pair, first, left] = part(q)
            ql[pair, first, right] = zero
            ql[pair, second, left] = part(qlap)
            ql[pair, second, right] = part(q)

    for h in range(HEADS):
        vt[h, 3 * HEAD :, :] = jnp.ones((16, 2 * ROWS), BF16)
    top_ref[...] = jnp.full(top_ref.shape, -1e30, F32)
    acc[...] = jnp.zeros(acc.shape, F32)
    sums[...] = jnp.zeros(sums.shape, F32)
    g_s[0, 0] = spin_own[...]
    spin_row = spin_own[...]

    def same_as(o, side):
        keys = jnp.transpose(jnp.broadcast_to(g_s[o, side], (ROWS, ROWS)))
        return jnp.where(keys == spin_row, 1.0, 0.0)

    def attend(o):
        x = g_l[o].reshape(2 * ROWS, WIDTH)
        x0 = g_t[o].reshape(2 * ROWS, WIDTH)
        x1 = g_r[o].reshape(2 * ROWS, WIDTH)
        for n, rows in enumerate((x, x0, x1)):
            keys = dot(rows, wk[...]).astype(BF16)
            for pair in range(2):
                kk[pair, n] = keys[:, pair * ROWS : (pair + 1) * ROWS]
            values = dot_t(wvt[...], rows).astype(BF16)
            place = (1, 0, 2)[n] * HEAD
            for h in range(HEADS):
                vt[h, place : place + HEAD, :] = values[h * HEAD : (h + 1) * HEAD]
        for side in range(2):
            rows = slice(side * ROWS, (side + 1) * ROWS)
            s_bias[rows] = g_b[o, side].astype(F32)
            s_same[rows] = same_as(o, side)

        def pair_step(pair, carry):
            k, k0, k1 = kk[pair, 0], kk[pair, 1], kk[pair, 2]
            ra = dot_t(jnp.concatenate([k, k0], 1), qa[pair])
            rb = dot_t(jnp.concatenate([k, k1], 1), qb[pair])
            rc = dot_t(jnp.concatenate([k0, k1], 1), qc[pair])
            for e in range(2):
                h = pair * 2 + e
                one = slice(e * ROWS, (e + 1) * ROWS)
                two = slice((2 + e) * ROWS, (3 + e) * ROWS)
                scores = ra[:, one] + hg_ref[h] * s_bias[...] + sg_ref[h] * s_same[...]
                t0, t1, c = ra[:, two], rb[:, one], rc[:, one]
                old = top_ref[h]
                top = jnp.maximum(old, jnp.max(scores, axis=0, keepdims=True))
                top_ref[h] = top
                shrink = jnp.exp(old - top)
                expo = jnp.exp(scores - top)
                e0 = expo * t0
                e1 = expo * t1
                e2 = e0 * t0 + e1 * t1 + expo * c
                w = expo.astype(BF16)
                w0 = e0.astype(BF16)
                w1 = e1.astype(BF16)
                w2 = e2.astype(BF16)
                p = dot(vt[h], jnp.concatenate([w, w0], 1))
                r = dot(vt[h, HEAD:, :], jnp.concatenate([w1, w2], 1))
                left, right = slice(0, ROWS), slice(ROWS, 2 * ROWS)
                a, b, d = slice(0, 64), slice(64, 128), slice(128, 192)
                acc[h, 0:64] = acc[h, 0:64] * shrink + p[b, left]
                acc[h, 64:128] = acc[h, 64:128] * shrink + (p[b, right] + p[a, left])
                acc[h, 128:192] = acc[h, 128:192] * shrink + (r[a, left] + p[d, left])
                acc[h, 192:256] = acc[h, 192:256] * shrink + (
                    r[a, right] + 2.0 * (p[a, right] + r[b, left])
                )
                sums[h, 0] = sums[h, 0] * shrink + p[192:200, left]
                sums[h, 1] = sums[h, 1] * shrink + p[192:200, right]
                sums[h, 2] = sums[h, 2] * shrink + r[128:136, left]
                sums[h, 3] = sums[h, 3] * shrink + r[128:136, right]
            return carry

        lax.fori_loop(0, 2, pair_step, 0)

    def offsets(step):
        return [step] if step == nz - step or step == 0 else [step, nz - step]

    def ring(step):
        if step == 0:
            cross_r.wait_recv()
            for o in next_of(0, last_up_r):
                start(flow_r(o, 1))
            return
        for o in arrivals(step, last_up):
            flow_t(o).wait_recv()
            for n in next_of(o, last_up):
                start(flow_t(n))
            start(cross_t(o))
            flow_l(o).wait_recv()
            for n in next_of(o, last_up):
                start(flow_l(n))
            start(cross_l(o))
            start(mate_l(o, 0))
        for side in range(2):
            for o in arrivals(step, last_up_r):
                flow_r(o, side).wait_recv()
                for n in next_of(o, last_up_r):
                    start(flow_r(n, side))

    def share(step):
        for o in offsets(step):
            cross_l(o).wait_recv()
            start(mate_l(o, 1))
            for side in range(2):
                if (o, side) != (0, 0):
                    direct_b(o, side).wait_recv()
                    start(mate_b(o, side))

    def use(step):
        for o in offsets(step):
            cross_t(o).wait_recv()
            for side in range(2):
                if (o, side) != (0, 0):
                    mate_l(o, side).wait_recv()
                    mate_b(o, side).wait_recv()
                    direct_s(o, side).wait_recv()
        choices = offsets(step)
        if len(choices) == 1:
            attend(choices[0])
        else:
            jump = choices[1] - choices[0]

            def one(n, carry):
                attend(choices[0] + n * jump)
                return carry

            lax.fori_loop(0, 2, one, 0)

    steps = nz // 2
    for step in range(steps + 1):
        ring(step)
        if step >= 1:
            share(step - 1)
        if step >= 2:
            use(step - 2)
    share(steps)
    use(steps - 1)
    use(steps)

    @pl.when(is_own)
    def _():
        copy_x_own.wait()

    @pl.when(jnp.logical_not(is_own))
    def _():
        copy_x.wait()

    lx = g_l[share_o, share_y, my_half]
    lk = dot(lx, wk[...]).astype(BF16)
    lv = dot_t(wvt[...], lx).astype(BF16)
    lk2 = dot(g_x[...], wk[...]).astype(BF16)
    lv2 = dot_t(wvt[...], g_x[...]).astype(BF16)
    lbias = g_b[share_o, share_y, my_half].astype(F32)
    s_spin[...] = same_as(share_o, share_y)
    lsame = s_spin[my_half]
    for pair in range(2):
        cols = slice(pair * ROWS, (pair + 1) * ROWS)
        res = dot_t(jnp.concatenate([lk[:, cols], lk2[:, cols]], 1), ql[pair])
        for e in range(2):
            h = pair * 2 + e
            scores = res[:, e * ROWS : (e + 1) * ROWS] + hg_ref[h] * lbias + sg_ref[h] * lsame
            expo = jnp.exp(scores - top_ref[h])
            w = expo.astype(BF16)
            wl = (expo * res[:, (2 + e) * ROWS : (3 + e) * ROWS]).astype(BF16)
            hrows = slice(h * HEAD, (h + 1) * HEAD)
            lnum = dot(lv[hrows], wl) + dot(lv2[hrows], w)
            lsum = jnp.sum(wl.astype(F32), axis=0, keepdims=True)
            inv = 1.0 / sums[h, 0, 0:1]
            td0 = sums[h, 1, 0:1]
            td1 = sums[h, 2, 0:1]
            trd = sums[h, 3, 0:1] + lsum
            attn = acc[h, 0:64] * inv
            at0 = (acc[h, 64:128] - attn * td0) * inv
            at1 = (acc[h, 128:192] - attn * td1) * inv
            term = (acc[h, 192:256] + lnum - attn * trd - 2.0 * (td0 * at0 + td1 * at1)) * inv
            a_attn[hrows] = attn
            a_tan[0, hrows] = at0
            a_tan[1, hrows] = at1
            own[h * 8 : (h + 1) * 8] = term.reshape(8, 8, ROWS)

    def rs_copy(k):
        there = (tan + k) % tans
        return remote(own.at[there], rs.at[k], rs_send.at[k], rs_recv.at[k], {"tan": there})

    def ag_copy(k):
        there = (tan + k) % tans
        return remote(red, ag.at[tan], ag_send.at[k], ag_recv.at[k], {"tan": there})

    def each(body):
        def run(k, carry):
            body(k)
            return carry

        lax.fori_loop(1, tans, run, 0)

    each(lambda k: rs_copy(k).start())

    def project_out(value, rows):
        flat = jnp.transpose(value).astype(BF16)
        return dot(flat, wo[...]) + rows.astype(F32)

    layer_out[...] = project_out(a_attn[...], g_l[0, 0]).astype(BF16)
    tan_out[0] = project_out(a_tan[0], g_t[0, 0]).astype(BF16)
    tan_out[1] = project_out(a_tan[1], g_r[0, 0]).astype(BF16)
    rs[0] = own[tan]

    each(lambda k: rs_copy(k).wait_recv())
    red[...] = jnp.sum(rs[...], axis=0)
    each(lambda k: ag_copy(k).start())
    ag[tan] = red[...]
    each(lambda k: rs_copy(k).wait_send())
    for copy in started:
        copy.wait_send()
    each(lambda k: ag_copy(k).wait_recv())
    lap_out[...] = project_out(ag[...].reshape(WIDTH, ROWS), lap_own[...])
    each(lambda k: ag_copy(k).wait_send())


def solution(mesh):
    blks, tans = mesh.shape["blk"], mesh.shape["tan"]
    nz = blks // 2

    def on_device(layer, lap, tangent, spin, bias, wq, wk, wv, wo, hg, sg):
        tangents = jnp.transpose(tangent, (1, 0, 2))
        spins = spin.astype(F32).reshape(1, ROWS)
        any_spec = pl.BlockSpec(memory_space=pl.ANY)
        smem = pl.BlockSpec(memory_space=pltpu.SMEM)
        vmem = pl.BlockSpec(memory_space=pltpu.VMEM)
        sq = (WIDTH, WIDTH)
        scratch = [
            pltpu.VMEM(sq, BF16),
            pltpu.VMEM(sq, BF16),
            pltpu.VMEM(sq, BF16),
            pltpu.VMEM(sq, BF16),
            pltpu.VMEM(sq, BF16),
            pltpu.VMEM((ROWS, WIDTH), BF16),
            pltpu.VMEM((1, ROWS), F32),
            pltpu.VMEM((nz, 2, ROWS, WIDTH), BF16),
            pltpu.VMEM((nz, 2, ROWS, WIDTH), BF16),
            pltpu.VMEM((nz, 2, ROWS, WIDTH), BF16),
            pltpu.VMEM((nz, 2, ROWS, ROWS), BF16),
            pltpu.VMEM((nz, 2, 1, ROWS), F32),
            pltpu.VMEM((HALF, WIDTH), BF16),
            pltpu.VMEM((2, 4 * ROWS, WIDTH), BF16),
            pltpu.VMEM((2, 2 * ROWS, WIDTH), BF16),
            pltpu.VMEM((2, 2 * ROWS, WIDTH), BF16),
            pltpu.VMEM((2, 4 * ROWS, WIDTH), BF16),
            pltpu.VMEM((2, 3, 2 * ROWS, ROWS), BF16),
            pltpu.VMEM((HEADS, 3 * HEAD + 16, 2 * ROWS), BF16),
            pltpu.VMEM((2 * ROWS, ROWS), F32),
            pltpu.VMEM((2 * ROWS, ROWS), F32),
            pltpu.VMEM((ROWS, ROWS), F32),
            pltpu.VMEM((HEADS, 1, ROWS), F32),
            pltpu.VMEM((HEADS, 4 * HEAD, ROWS), F32),
            pltpu.VMEM((HEADS, 4, 8, ROWS), F32),
            pltpu.VMEM((WIDTH, ROWS), F32),
            pltpu.VMEM((2, WIDTH, ROWS), F32),
            pltpu.VMEM((tans, WIDTH // tans, ROWS), F32),
            pltpu.VMEM((tans, WIDTH // tans, ROWS), F32),
            pltpu.VMEM((WIDTH // tans, ROWS), F32),
            pltpu.VMEM((tans, WIDTH // tans, ROWS), F32),
            pltpu.SemaphoreType.DMA((11,)),
        ]
        one, two = (nz,), (nz, 2)
        for shape in (one, one, one, one, two, two, (1,), two, two, two, (1,), (tans,), (tans,)):
            scratch += [pltpu.SemaphoreType.DMA(shape)] * 2
        layer_out, tan_out, lap_out = pl.pallas_call(
            functools.partial(kernel, nz, tans),
            out_shape=(
                jax.ShapeDtypeStruct((ROWS, WIDTH), BF16),
                jax.ShapeDtypeStruct((2, ROWS, WIDTH), BF16),
                jax.ShapeDtypeStruct((ROWS, WIDTH), F32),
            ),
            in_specs=[any_spec] * 9 + [smem, smem],
            out_specs=(vmem, vmem, vmem),
            scratch_shapes=scratch,
            compiler_params=pltpu.CompilerParams(collective_id=0, has_side_effects=True),
            name="laplacian_attention",
        )(layer, lap, tangents, spins, bias, wq, wk, wv, wo, hg, sg)
        return layer_out, jnp.transpose(tan_out, (1, 0, 2)), lap_out

    in_specs = (
        P("blk", None),
        P("blk", None),
        P("blk", "tan", None),
        P("blk"),
        P("blk", None),
        P(),
        P(),
        P(),
        P(),
        P(),
        P(),
    )
    out_specs = (P("blk", None), P("blk", "tan", None), P("blk", None))
    return jax.shard_map(
        on_device, mesh=mesh, in_specs=in_specs, out_specs=out_specs, check_vma=False
    )
```

```python
import functools

import jax
import jax.numpy as jnp
from jax import lax
from jax.experimental import pallas as pl
from jax.experimental.pallas import tpu as pltpu
from jax.sharding import PartitionSpec as P

MESH = pl.DeviceIdType.MESH
F32 = jnp.float32
BF16 = jnp.bfloat16
ROWS = 128
HALF = 64
SHARE = 16
WIDTH = 256
HEADS = 4
HEAD = 64
NX = 4
PEERS = 16


def dot(a, b):
    return jnp.dot(a, b, preferred_element_type=F32)


def dot_t(a, b):
    return lax.dot_general(a, b, (((1,), (1,)), ((), ())), preferred_element_type=F32)


def kernel(
    nz,
    tans,
    layer_hbm,
    lap_hbm,
    tan_hbm,
    spin_hbm,
    bias_hbm,
    wq_hbm,
    wk_hbm,
    wv_hbm,
    wo_hbm,
    hg_ref,
    sg_ref,
    layer_out,
    tan_out,
    lap_out,
    wq,
    wk,
    wv,
    wo,
    wvt,
    lap_own,
    tan_own,
    g_lb,
    g_t,
    g_s,
    g_x,
    qa,
    ql,
    lhs,
    vt,
    s_bias,
    s_same,
    s_spin,
    top_ref,
    acc,
    sums,
    a_attn,
    a_tan,
    a_term,
    own,
    rs,
    red,
    high,
    ag,
    back_out,
    back_in,
    local_sem,
    d_l_send,
    d_l_recv,
    d_b_send,
    d_b_recv,
    d_s_send,
    d_s_recv,
    y_send,
    y_recv,
    ys_send,
    ys_recv,
    x_send,
    x_recv,
    c_send,
    c_recv,
    t_send,
    t_recv,
    o_send,
    o_recv,
    rs_send,
    rs_recv,
    h_send,
    h_recv,
    ag_send,
    ag_recv,
):
    blk = lax.axis_index("blk")
    tan = lax.axis_index("tan")
    z = blk // 2
    y = blk % 2
    core = tan % 2
    x = (tan // 2) % NX
    high_y = tan // (2 * NX)
    highs = tans // (2 * NX)
    member = core * NX + x
    me = y * (PEERS // 2) + member
    share = pl.ds(pl.multiple_of(member * SHARE, SHARE), SHARE)
    my_half = pl.ds(pl.multiple_of(core * HALF, HALF), HALF)
    own_lanes = pl.ds(pl.multiple_of(y * ROWS, ROWS), ROWS)

    def tan_of(high_at, x_at, core_at):
        return (high_at * NX + x_at) * 2 + core_at

    def group(k):
        at = (me + k) % PEERS
        inner = at % (PEERS // 2)
        return at // (PEERS // 2), inner

    def group_id(k):
        side, inner = group(k)
        return {"blk": z * 2 + side, "tan": tan_of(high_y, inner % NX, inner // NX)}

    def z_id(k):
        return {"blk": ((z + k) % nz) * 2 + y}

    def high_id(k):
        return {"tan": tan_of((high_y + k) % highs, x, core)}

    share_o = tan // 4
    share_y = (tan // 2) % 2
    is_own = tan < 2
    not_own = jnp.logical_not(is_own)
    share_to = ((z + share_o) % nz) * 2 + (y + share_y) % 2
    share_from = ((z + nz - share_o) % nz) * 2 + (y + share_y) % 2

    barrier = pltpu.get_barrier_semaphore()

    def loop(first, last, body):
        def run(k, carry):
            body(k)
            return carry

        lax.fori_loop(first, last, run, 0)

    def greet(device):
        pl.semaphore_signal(barrier, inc=1, device_id=device, device_id_type=MESH)

    loop(1, nz, lambda k: greet(z_id(k)))
    loop(1, PEERS, lambda k: greet(group_id(k)))
    loop(1, highs, lambda k: greet(high_id(k)))

    @pl.when(not_own)
    def _():
        greet({"blk": share_from})

    pair_cols = pl.ds(pl.multiple_of(z * 2 * ROWS, 2 * ROWS), 2 * ROWS)
    local = [
        (tan_hbm.at[y], g_t.at[0, 0]),
        (layer_hbm, g_lb.at[0, 0, 0]),
        (bias_hbm.at[:, pair_cols], g_lb.at[0, 0, 1]),
        (spin_hbm, g_s.at[0, 0]),
        (wq_hbm, wq),
        (wk_hbm, wk),
        (wv_hbm, wv),
        (lap_hbm, lap_own),
        (tan_hbm.at[1 - y], tan_own),
        (wo_hbm, wo),
    ]
    local = [
        pltpu.make_async_copy(src, dst, local_sem.at[n]) for n, (src, dst) in enumerate(local)
    ]
    for copy in local:
        copy.start()

    other_y = {"blk": z * 2 + (1 - y)}
    other_core = {"tan": tan + 1 - 2 * core}
    started = []

    def remote(src, dst, send, recv, device):
        return pltpu.make_async_remote_copy(
            src_ref=src,
            dst_ref=dst,
            send_sem=send,
            recv_sem=recv,
            device_id=device,
            device_id_type=MESH,
        )

    def start(copy):
        copy.start()
        started.append(copy)

    def direct_l(o):
        there = z_id(o)
        return remote(
            layer_hbm.at[share], g_lb.at[o, 0, 0, share], d_l_send.at[o], d_l_recv.at[o], there
        )

    def direct_b(o):
        there = (z + o) % nz
        columns = pl.ds(pl.multiple_of(there * 2 * ROWS, 2 * ROWS), 2 * ROWS)
        return remote(
            bias_hbm.at[share, columns],
            g_lb.at[o, 0, 1, share],
            d_b_send.at[o],
            d_b_recv.at[o],
            z_id(o),
        )

    def direct_s(o):
        return remote(spin_hbm, g_s.at[o, 0], d_s_send.at[o], d_s_recv.at[o], z_id(o))

    def cross(o):
        return remote(
            g_lb.at[o, 0, :, share],
            g_lb.at[o, 1, :, share],
            y_send.at[o],
            y_recv.at[o],
            other_y,
        )

    def cross_s(o):
        return remote(g_s.at[o, 0], g_s.at[o, 1], ys_send.at[o], ys_recv.at[o], other_y)

    def spread(o, k):
        piece = g_lb.at[o, 1, :, share] if o == 0 else g_lb.at[o, :, :, share]
        device = {"tan": tan_of(high_y, (x + k) % NX, core)}
        return remote(piece, piece, x_send.at[o, k], x_recv.at[o, k], device)

    def mate(o):
        piece = g_lb.at[o, 1, :, my_half] if o == 0 else g_lb.at[o, :, :, my_half]
        return remote(piece, piece, c_send.at[o], c_recv.at[o], other_core)

    cross_t = remote(tan_hbm.at[1 - y], g_t.at[0, 1], o_send.at[0], o_recv.at[0], other_y)

    def last_up(side):
        return nz // 2 if side == 0 else nz - 1 - nz // 2

    def flow(o, side):
        if o <= last_up(side):
            src, device = o - 1, z_id(1)
        else:
            src, device = (o + 1) % nz, z_id(nz - 1)
        return remote(
            g_t.at[src, side], g_t.at[o, side], t_send.at[o, side], t_recv.at[o, side], device
        )

    def next_of(o, side):
        last = last_up(side)
        if o == 0:
            return [n for n in sorted({1, nz - 1}) if n <= 1 or n > last]
        if o <= last:
            return [o + 1] if o < last else []
        return [o - 1] if o - 1 > last else []

    def offsets(step):
        return sorted({step, (nz - step) % nz})

    copy_x = remote(lap_hbm.at[my_half], g_x, o_send.at[1], o_recv.at[1], {"blk": share_to})
    copy_x_own = pltpu.make_async_copy(lap_hbm.at[my_half], g_x, local_sem.at[10])

    for copy in local[:4]:
        copy.wait()
    greeted = nz - 1 + PEERS - 1 + highs - 1
    pl.semaphore_wait(barrier, greeted + jnp.where(is_own, 0, 1))

    steps = nz // 2
    start(cross_t)
    start(cross(0))
    start(cross_s(0))
    for step in range(1, steps + 1):
        for o in offsets(step):
            start(direct_l(o))
            start(direct_b(o))
            start(direct_s(o))
        if step == 1:
            for o in next_of(0, 0):
                start(flow(o, 0))

    @pl.when(is_own)
    def _():
        copy_x_own.start()

    @pl.when(not_own)
    def _():
        copy_x.start()

    for copy in local[4:]:
        copy.wait()

    lanes = lax.broadcasted_iota(jnp.int32, (ROWS, ROWS), 1)
    left, right = slice(0, ROWS), slice(ROWS, 2 * ROWS)

    def queries(rows):
        return dot(rows, wq[...]).astype(BF16).astype(F32) * 0.125

    def masked(value, h, scale=1.0):
        pair, e = h // 2, h % 2
        keep = (lanes >= e * HEAD) & (lanes < (e + 1) * HEAD)
        return jnp.where(keep, value[:, pair * ROWS : (pair + 1) * ROWS] * scale, 0.0).astype(BF16)

    zero = jnp.zeros((ROWS, ROWS), BF16)

    def prepare(side):
        at = (y + side) % 2
        q = queries(g_lb[0, side, 0])
        qt = queries(g_t[0, side])

        def rows(n):
            return pl.ds(pl.multiple_of(n * 2 * ROWS + at * ROWS, ROWS), ROWS)

        for h in range(HEADS):
            qh = masked(q, h)
            qa[h, rows(0), left] = qh
            qa[h, rows(0), right] = zero
            qa[h, rows(1), left] = masked(qt, h)
            qa[h, rows(1), right] = qh
            qa[h, rows(2), left] = zero
            qa[h, rows(2), right] = masked(qt, h, 2.0)
        return q

    def prepare_own():
        q = prepare(0)
        qlap = queries(lap_own[...])
        for h in range(HEADS):
            first = slice((h % 2) * ROWS, (h % 2 + 1) * ROWS)
            second = slice((2 + h % 2) * ROWS, (3 + h % 2) * ROWS)
            qh = masked(q, h)
            ql[h // 2, first, left] = qh
            ql[h // 2, first, right] = zero
            ql[h // 2, second, left] = masked(qlap, h)
            ql[h // 2, second, right] = qh
        wvt[...] = jnp.transpose(wv[...].astype(F32)).astype(BF16)
        for h in range(HEADS):
            vt[h, 2 * HEAD :, :] = jnp.ones((16, 2 * ROWS), BF16)
        top_ref[...] = jnp.full(top_ref.shape, -1e30, F32)
        acc[...] = jnp.zeros(acc.shape, F32)
        sums[...] = jnp.zeros(sums.shape, F32)

    def spin_of(o, side):
        return jnp.transpose(jnp.broadcast_to(g_s[o, side].astype(F32), (ROWS, ROWS)))

    def attend(o):
        for n in range(2):
            if n == 0:
                rows = jnp.concatenate([g_lb[o, 0, 0], g_lb[o, 1, 0]], 0)
            else:
                rows = g_t[o].reshape(2 * ROWS, WIDTH)
            keys = dot(rows, wk[...]).astype(BF16)
            for pair in range(2):
                lhs[pair, :, n * ROWS : (n + 1) * ROWS] = keys[:, pair * ROWS : (pair + 1) * ROWS]
            values = dot_t(wvt[...], rows).astype(BF16)
            place = (1 - n) * HEAD
            for h in range(HEADS):
                vt[h, place : place + HEAD, :] = values[h * HEAD : (h + 1) * HEAD]
        for side in range(2):
            rows = slice(side * ROWS, (side + 1) * ROWS)
            s_bias[rows] = g_lb[o, side, 1].astype(F32)
            keys = spin_of(o, side)
            for half in range(2):
                row = g_s[0, (y + half) % 2].astype(F32)
                s_same[rows, half * ROWS : (half + 1) * ROWS] = jnp.where(keys == row, 1.0, 0.0)

        def head_step(h, carry):
            res = dot_t(lhs[h // 2], qa[h])
            wide = 2 * ROWS
            scores = res[:, :wide] + hg_ref[h] * s_bias[...] + sg_ref[h] * s_same[...]
            t, c = res[:, wide : 2 * wide], res[:, 2 * wide :]
            old = top_ref[h]
            top = jnp.maximum(old, jnp.max(scores, axis=0, keepdims=True))
            top_ref[h] = top
            shrink = jnp.exp(old - top)
            expo = jnp.exp(scores - top)
            e1 = expo * t
            e2 = e1 * t + expo * c
            w = expo.astype(BF16)
            w1 = e1.astype(BF16)
            w2 = e2.astype(BF16)
            p = dot(vt[h], jnp.concatenate([w, w1], 1))
            r = dot(vt[h, HEAD:, :], w2)
            a, b = slice(0, 64), slice(64, 128)
            one, two = slice(0, wide), slice(wide, 2 * wide)
            acc[h, 0:64] = acc[h, 0:64] * shrink + p[b, one]
            acc[h, 64:128] = acc[h, 64:128] * shrink + (p[b, two] + p[a, one])
            acc[h, 128:192] = acc[h, 128:192] * shrink + (r[a] + 2.0 * p[a, two])
            sums[h, 0] = sums[h, 0] * shrink + p[128:136, one]
            sums[h, 1] = sums[h, 1] * shrink + p[128:136, two]
            sums[h, 2] = sums[h, 2] * shrink + r[64:72]
            return carry

        lax.fori_loop(0, HEADS, head_step, 0)

    def pass_t(step, side):
        for o in offsets(step):
            if step == 0:
                cross_t.wait_recv()
            else:
                flow(o, side).wait_recv()
            for n in next_of(o, side):
                start(flow(n, side))

    def pass_y(step):
        for o in offsets(step):
            direct_l(o).wait_recv()
            direct_b(o).wait_recv()
            start(cross(o))
            direct_s(o).wait_recv()
            start(cross_s(o))

    def pass_x(step):
        for o in offsets(step):
            cross(o).wait_recv()
            for k in (1, 3, 2):
                start(spread(o, k))

    def pass_core(step):
        for o in offsets(step):
            for k in (1, 3, 2):
                spread(o, k).wait_recv()
            start(mate(o))

    def use(step):
        choices = offsets(step)
        for o in choices:
            cross_s(o).wait_recv()
            mate(o).wait_recv()
        if step == 0:
            prepare(1)
        if len(choices) == 1:
            attend(choices[0])
        else:
            jump = choices[1] - choices[0]

            def one(n, carry):
                attend(choices[0] + n * jump)
                return carry

            lax.fori_loop(0, 2, one, 0)

    pass_t(0, 1)
    prepare_own()
    pass_x(0)
    pass_y(1)
    pass_t(1, 0)
    pass_t(1, 1)
    for step in range(2, steps + 1):
        pass_y(step)
    pass_x(1)
    pass_core(0)
    pass_t(2, 0)
    pass_t(2, 1)
    for step in range(2, steps + 1):
        pass_x(step)
    pass_core(1)
    use(0)
    pass_t(3, 0)
    pass_t(3, 1)
    for step in range(2, steps + 1):
        pass_core(step)
    use(1)
    use(2)
    use(3)
    pass_t(4, 0)
    pass_t(4, 1)
    use(4)

    @pl.when(is_own)
    def _():
        copy_x_own.wait()

    @pl.when(not_own)
    def _():
        copy_x.wait()

    lx = g_lb[share_o, share_y, 0, my_half]
    lk = dot(lx, wk[...]).astype(BF16)
    lv = dot_t(wvt[...], lx).astype(BF16)
    lk2 = dot(g_x[...], wk[...]).astype(BF16)
    lv2 = dot_t(wvt[...], g_x[...]).astype(BF16)
    lbias = g_lb[share_o, share_y, 1, my_half, own_lanes].astype(F32)
    s_spin[...] = jnp.where(spin_of(share_o, share_y) == g_s[0, 0].astype(F32), 1.0, 0.0)
    lsame = s_spin[my_half]
    for h in range(HEADS):
        inv = 1.0 / sums[h, 0, 0:1]
        td = sums[h, 1, 0:1]
        attn = acc[h, 0:64] * inv
        at = (acc[h, 64:128] - attn * td) * inv
        hrows = slice(h * HEAD, (h + 1) * HEAD)
        a_attn[hrows] = attn
        a_tan[hrows] = at
        a_term[hrows] = (acc[h, 128:192] - attn * sums[h, 2, 0:1] - 2.0 * td * at) * inv
    for pair in range(2):
        cols = slice(pair * ROWS, (pair + 1) * ROWS)
        res = dot_t(jnp.concatenate([lk[:, cols], lk2[:, cols]], 1), ql[pair])
        for e in range(2):
            h = pair * 2 + e
            scores = res[:, e * ROWS : (e + 1) * ROWS] + hg_ref[h] * lbias + sg_ref[h] * lsame
            expo = jnp.exp(scores - top_ref[h, :, own_lanes])
            w = expo.astype(BF16)
            wl = (expo * res[:, (2 + e) * ROWS : (3 + e) * ROWS]).astype(BF16)
            hrows = slice(h * HEAD, (h + 1) * HEAD)
            lnum = dot(lv[hrows], wl) + dot(lv2[hrows], w)
            lsum = jnp.sum(wl.astype(F32), axis=0, keepdims=True)
            inv = 1.0 / sums[h, 0, 0:1, own_lanes]
            a_term[hrows, own_lanes] += (lnum - a_attn[hrows, own_lanes] * lsum) * inv

    for side in range(2):
        terms = a_term[:, side * ROWS : (side + 1) * ROWS].astype(BF16)
        own[side] = terms.reshape(PEERS // 2, 2 * SHARE, ROWS)

    def rs_copy(k):
        side, inner = group(k)
        return remote(own.at[side, inner], rs.at[k], rs_send.at[k], rs_recv.at[k], group_id(k))

    def high_copy(k):
        return remote(red, high.at[high_y], h_send.at[k], h_recv.at[k], high_id(k))

    def ag_copy(k):
        inner = (member + k) % (PEERS // 2)
        device = {"tan": tan_of(high_y, inner % NX, inner // NX)}
        return remote(ag.at[member], ag.at[member], ag_send.at[k], ag_recv.at[k], device)

    def project_out(value, rows):
        flat = jnp.transpose(value).astype(BF16)
        return dot(flat, wo[...]) + rows.astype(F32)

    loop(1, PEERS, lambda k: rs_copy(k).start())
    other_lanes = pl.ds(pl.multiple_of((1 - y) * ROWS, ROWS), ROWS)
    back_out[...] = project_out(a_tan[:, other_lanes], g_t[0, 1]).astype(BF16)
    copy_back = remote(back_out, back_in, o_send.at[2], o_recv.at[2], other_y)
    copy_back.start()
    rs[0] = own[y, member]
    loop(1, PEERS, lambda k: rs_copy(k).wait_recv())
    red[...] = jnp.sum(rs[...].astype(F32), axis=0).astype(BF16)
    loop(1, highs, lambda k: high_copy(k).start())
    layer_out[...] = project_out(a_attn[:, own_lanes], g_lb[0, 0, 0]).astype(BF16)
    tan_out[y] = project_out(a_tan[:, own_lanes], g_t[0, 0]).astype(BF16)
    high[high_y] = red[...]
    loop(1, highs, lambda k: high_copy(k).wait_recv())
    ag[member] = jnp.sum(high[...].astype(F32), axis=0).astype(BF16)
    loop(1, PEERS // 2, lambda k: ag_copy(k).start())
    copy_back.wait_recv()
    tan_out[1 - y] = back_in[...]
    for copy in started:
        copy.wait_send()
    copy_back.wait_send()
    loop(1, PEERS, lambda k: rs_copy(k).wait_send())
    loop(1, highs, lambda k: high_copy(k).wait_send())
    loop(1, PEERS // 2, lambda k: ag_copy(k).wait_recv())
    lap_out[...] = project_out(ag[...].reshape(WIDTH, ROWS).astype(F32), lap_own[...])
    loop(1, PEERS // 2, lambda k: ag_copy(k).wait_send())


def solution(mesh):
    blks, tans = mesh.shape["blk"], mesh.shape["tan"]
    nz = blks // 2

    def on_device(layer, lap, tangent, spin, bias, wq, wk, wv, wo, hg, sg):
        tangents = jnp.transpose(tangent, (1, 0, 2))
        spins = spin.reshape(1, ROWS)
        any_spec = pl.BlockSpec(memory_space=pl.ANY)
        smem = pl.BlockSpec(memory_space=pltpu.SMEM)
        vmem = pl.BlockSpec(memory_space=pltpu.VMEM)
        sq = (WIDTH, WIDTH)
        scratch = [
            pltpu.VMEM(sq, BF16),
            pltpu.VMEM(sq, BF16),
            pltpu.VMEM(sq, BF16),
            pltpu.VMEM(sq, BF16),
            pltpu.VMEM(sq, BF16),
            pltpu.VMEM((ROWS, WIDTH), BF16),
            pltpu.VMEM((ROWS, WIDTH), BF16),
            pltpu.VMEM((nz, 2, 2, ROWS, WIDTH), BF16),
            pltpu.VMEM((nz, 2, ROWS, WIDTH), BF16),
            pltpu.VMEM((nz, 2, 1, ROWS), jnp.int32),
            pltpu.VMEM((HALF, WIDTH), BF16),
            pltpu.VMEM((HEADS, 6 * ROWS, WIDTH), BF16),
            pltpu.VMEM((2, 4 * ROWS, WIDTH), BF16),
            pltpu.VMEM((2, 2 * ROWS, WIDTH), BF16),
            pltpu.VMEM((HEADS, 2 * HEAD + 16, 2 * ROWS), BF16),
            pltpu.VMEM((2 * ROWS, 2 * ROWS), F32),
            pltpu.VMEM((2 * ROWS, 2 * ROWS), F32),
            pltpu.VMEM((ROWS, ROWS), F32),
            pltpu.VMEM((HEADS, 1, 2 * ROWS), F32),
            pltpu.VMEM((HEADS, 3 * HEAD, 2 * ROWS), F32),
            pltpu.VMEM((HEADS, 3, 8, 2 * ROWS), F32),
            pltpu.VMEM((WIDTH, 2 * ROWS), F32),
            pltpu.VMEM((WIDTH, 2 * ROWS), F32),
            pltpu.VMEM((WIDTH, 2 * ROWS), F32),
            pltpu.VMEM((2, PEERS // 2, 2 * SHARE, ROWS), BF16),
            pltpu.VMEM((PEERS, 2 * SHARE, ROWS), BF16),
            pltpu.VMEM((2 * SHARE, ROWS), BF16),
            pltpu.VMEM((tans // (2 * NX), 2 * SHARE, ROWS), BF16),
            pltpu.VMEM((PEERS // 2, 2 * SHARE, ROWS), BF16),
            pltpu.VMEM((ROWS, WIDTH), BF16),
            pltpu.VMEM((ROWS, WIDTH), BF16),
            pltpu.SemaphoreType.DMA((11,)),
        ]
        one, two = (nz,), (nz, 2)
        shapes = (one, one, one, one, one, (nz, NX), one, two, (3,))
        for shape in shapes + ((PEERS,), (tans // (2 * NX),), (PEERS // 2,)):
            scratch += [pltpu.SemaphoreType.DMA(shape)] * 2
        layer_out, tan_out, lap_out = pl.pallas_call(
            functools.partial(kernel, nz, tans),
            out_shape=(
                jax.ShapeDtypeStruct((ROWS, WIDTH), BF16),
                jax.ShapeDtypeStruct((2, ROWS, WIDTH), BF16),
                jax.ShapeDtypeStruct((ROWS, WIDTH), F32),
            ),
            in_specs=[any_spec] * 9 + [smem, smem],
            out_specs=(vmem, vmem, vmem),
            scratch_shapes=scratch,
            compiler_params=pltpu.CompilerParams(collective_id=0, has_side_effects=True),
            name="laplacian_attention",
        )(layer, lap, tangents, spins, bias, wq, wk, wv, wo, hg, sg)
        return layer_out, jnp.transpose(tan_out, (1, 0, 2)), lap_out

    in_specs = (
        P("blk", None),
        P("blk", None),
        P("blk", "tan", None),
        P("blk"),
        P("blk", None),
        P(),
        P(),
        P(),
        P(),
        P(),
        P(),
    )
    out_specs = (P("blk", None), P("blk", "tan", None), P("blk", None))
    return jax.shard_map(
        on_device, mesh=mesh, in_specs=in_specs, out_specs=out_specs, check_vma=False
    )
```

```python
import functools

import jax
import jax.numpy as jnp
from jax import lax
from jax.experimental import pallas as pl
from jax.experimental.pallas import tpu as pltpu
from jax.sharding import PartitionSpec as P

MESH = pl.DeviceIdType.MESH
F32 = jnp.float32
BF16 = jnp.bfloat16
ROWS = 128
HALF = 64
SHARE = 16
WIDTH = 256
HEADS = 4
HEAD = 64
NX = 4
PEERS = 16


def dot(a, b):
    return jnp.dot(a, b, preferred_element_type=F32)


def dot_t(a, b):
    return lax.dot_general(a, b, (((1,), (1,)), ((), ())), preferred_element_type=F32)


def kernel(
    nz,
    tans,
    layer_hbm,
    lap_hbm,
    tan_hbm,
    spin_hbm,
    bias_hbm,
    wq_hbm,
    wk_hbm,
    wv_hbm,
    wo_hbm,
    hg_ref,
    sg_ref,
    layer_out,
    tan_out,
    lap_out,
    wq,
    wk,
    wv,
    wo,
    wvt,
    lap_own,
    tan_own,
    tan_raw,
    g_lb,
    g_t,
    g_s,
    g_x,
    qa,
    ql,
    lhs,
    vt,
    s_bias,
    s_score,
    s_w,
    s_same,
    s_spin,
    top_ref,
    acc,
    sums,
    a_attn,
    a_tan,
    a_term,
    own,
    rs,
    red,
    high,
    ag,
    back_out,
    back_in,
    local_sem,
    d_l_send,
    d_l_recv,
    d_b_send,
    d_b_recv,
    d_s_send,
    d_s_recv,
    y_send,
    y_recv,
    ys_send,
    ys_recv,
    x_send,
    x_recv,
    c_send,
    c_recv,
    t_send,
    t_recv,
    o_send,
    o_recv,
    rs_send,
    rs_recv,
    h_send,
    h_recv,
    ag_send,
    ag_recv,
):
    blk = lax.axis_index("blk")
    tan = lax.axis_index("tan")
    z = blk // 2
    y = blk % 2
    core = tan % 2
    x = (tan // 2) % NX
    high_y = tan // (2 * NX)
    highs = tans // (2 * NX)
    member = core * NX + x
    me = y * (PEERS // 2) + member
    share = pl.ds(pl.multiple_of(member * SHARE, SHARE), SHARE)
    my_half = pl.ds(pl.multiple_of(core * HALF, HALF), HALF)
    own_lanes = pl.ds(pl.multiple_of(y * ROWS, ROWS), ROWS)

    def tan_of(high_at, x_at, core_at):
        return (high_at * NX + x_at) * 2 + core_at

    def group(k):
        at = (me + k) % PEERS
        inner = at % (PEERS // 2)
        return at // (PEERS // 2), inner

    def group_id(k):
        side, inner = group(k)
        return {"blk": z * 2 + side, "tan": tan_of(high_y, inner % NX, inner // NX)}

    def z_id(k):
        return {"blk": ((z + k) % nz) * 2 + y}

    def high_id(k):
        return {"tan": tan_of((high_y + k) % highs, x, core)}

    share_o = tan // 4
    share_y = (tan // 2) % 2
    is_own = tan < 2
    not_own = jnp.logical_not(is_own)
    share_to = ((z + share_o) % nz) * 2 + (y + share_y) % 2
    share_from = ((z + nz - share_o) % nz) * 2 + (y + share_y) % 2

    barrier = pltpu.get_barrier_semaphore()

    def loop(first, last, body):
        def run(k, carry):
            body(k)
            return carry

        lax.fori_loop(first, last, run, 0)

    def greet(device):
        pl.semaphore_signal(barrier, inc=1, device_id=device, device_id_type=MESH)

    loop(1, nz, lambda k: greet(z_id(k)))
    loop(1, PEERS, lambda k: greet(group_id(k)))
    loop(1, highs, lambda k: greet(high_id(k)))

    @pl.when(not_own)
    def _():
        greet({"blk": share_from})

    pair_cols = pl.ds(pl.multiple_of(z * 2 * ROWS, 2 * ROWS), 2 * ROWS)
    local = [
        (tan_hbm, tan_raw),
        (layer_hbm, g_lb.at[0, 0, 0]),
        (bias_hbm.at[:, pair_cols], g_lb.at[0, 0, 1]),
        (spin_hbm, g_s.at[0, 0]),
        (wq_hbm, wq),
        (wk_hbm, wk),
        (wv_hbm, wv),
        (lap_hbm, lap_own),
        (wo_hbm, wo),
    ]
    local = [
        pltpu.make_async_copy(src, dst, local_sem.at[n]) for n, (src, dst) in enumerate(local)
    ]
    for copy in local:
        copy.start()

    other_y = {"blk": z * 2 + (1 - y)}
    other_core = {"tan": tan + 1 - 2 * core}
    started = []

    def remote(src, dst, send, recv, device):
        return pltpu.make_async_remote_copy(
            src_ref=src,
            dst_ref=dst,
            send_sem=send,
            recv_sem=recv,
            device_id=device,
            device_id_type=MESH,
        )

    def start(copy):
        copy.start()
        started.append(copy)

    def direct_l(o):
        there = z_id(o)
        return remote(
            layer_hbm.at[share], g_lb.at[o, 0, 0, share], d_l_send.at[o], d_l_recv.at[o], there
        )

    def direct_b(o):
        there = (z + o) % nz
        columns = pl.ds(pl.multiple_of(there * 2 * ROWS, 2 * ROWS), 2 * ROWS)
        return remote(
            bias_hbm.at[share, columns],
            g_lb.at[o, 0, 1, share],
            d_b_send.at[o],
            d_b_recv.at[o],
            z_id(o),
        )

    def direct_s(o):
        return remote(spin_hbm, g_s.at[o, 0], d_s_send.at[o], d_s_recv.at[o], z_id(o))

    def cross(o):
        if o == 0:
            return remote(g_lb.at[0, 0], g_lb.at[0, 1], y_send.at[0], y_recv.at[0], other_y)
        return remote(
            g_lb.at[o, 0, :, share],
            g_lb.at[o, 1, :, share],
            y_send.at[o],
            y_recv.at[o],
            other_y,
        )

    def cross_s(o):
        return remote(g_s.at[o, 0], g_s.at[o, 1], ys_send.at[o], ys_recv.at[o], other_y)

    def spread(o, k):
        piece = g_lb.at[o, :, :, share]
        device = {"tan": tan_of(high_y, (x + k) % NX, core)}
        return remote(piece, piece, x_send.at[o, k], x_recv.at[o, k], device)

    def mate(o):
        piece = g_lb.at[o, :, :, my_half]
        return remote(piece, piece, c_send.at[o], c_recv.at[o], other_core)

    cross_t = remote(tan_own, g_t.at[0, 1], o_send.at[0], o_recv.at[0], other_y)

    def last_up(side):
        return nz // 2 if side == 0 else nz - 1 - nz // 2

    def flow(o, side):
        if o <= last_up(side):
            src, device = o - 1, z_id(1)
        else:
            src, device = (o + 1) % nz, z_id(nz - 1)
        return remote(
            g_t.at[src, side], g_t.at[o, side], t_send.at[o, side], t_recv.at[o, side], device
        )

    def next_of(o, side):
        last = last_up(side)
        if o == 0:
            return [n for n in sorted({1, nz - 1}) if n <= 1 or n > last]
        if o <= last:
            return [o + 1] if o < last else []
        return [o - 1] if o - 1 > last else []

    def offsets(step):
        return sorted({step, (nz - step) % nz})

    copy_x = remote(lap_hbm.at[my_half], g_x, o_send.at[1], o_recv.at[1], {"blk": share_to})
    copy_x_own = pltpu.make_async_copy(lap_hbm.at[my_half], g_x, local_sem.at[9])

    for copy in local[:4]:
        copy.wait()
    raw = tan_raw[...].astype(F32)
    first, second = raw[:, 0].astype(BF16), raw[:, 1].astype(BF16)
    g_t[0, 0] = jnp.where(y == 0, first, second)
    tan_own[...] = jnp.where(y == 0, second, first)
    greeted = nz - 1 + PEERS - 1 + highs - 1
    pl.semaphore_wait(barrier, greeted + jnp.where(is_own, 0, 1))

    steps = nz // 2
    start(cross_t)
    start(cross(0))
    start(cross_s(0))
    for step in range(1, steps + 1):
        for o in offsets(step):
            start(direct_l(o))
            start(direct_b(o))
            start(direct_s(o))
        if step == 1:
            for o in next_of(0, 0):
                start(flow(o, 0))

    @pl.when(is_own)
    def _():
        copy_x_own.start()

    @pl.when(not_own)
    def _():
        copy_x.start()

    for copy in local[4:]:
        copy.wait()

    lanes = lax.broadcasted_iota(jnp.int32, (ROWS, ROWS), 1)
    left, right = slice(0, ROWS), slice(ROWS, 2 * ROWS)

    def queries(rows):
        return dot(rows, wq[...]).astype(BF16).astype(F32) * 0.125

    def masked(value, h, scale=1.0):
        pair, e = h // 2, h % 2
        keep = (lanes >= e * HEAD) & (lanes < (e + 1) * HEAD)
        return jnp.where(keep, value[:, pair * ROWS : (pair + 1) * ROWS] * scale, 0.0).astype(BF16)

    zero = jnp.zeros((ROWS, ROWS), BF16)

    def prepare(side):
        at = (y + side) % 2
        q = queries(g_lb[0, side, 0])
        qt = queries(g_t[0, side])

        def rows(n):
            return pl.ds(pl.multiple_of(n * 2 * ROWS + at * ROWS, ROWS), ROWS)

        for h in range(HEADS):
            qh = masked(q, h)
            qa[h, rows(0), left] = qh
            qa[h, rows(0), right] = zero
            qa[h, rows(1), left] = masked(qt, h)
            qa[h, rows(1), right] = qh
            qa[h, rows(2), left] = zero
            qa[h, rows(2), right] = masked(qt, h, 2.0)
        return q

    def prepare_own():
        q = prepare(0)
        qlap = queries(lap_own[...])
        for h in range(HEADS):
            first = slice((h % 2) * ROWS, (h % 2 + 1) * ROWS)
            second = slice((2 + h % 2) * ROWS, (3 + h % 2) * ROWS)
            qh = masked(q, h)
            ql[h // 2, first, left] = qh
            ql[h // 2, first, right] = zero
            ql[h // 2, second, left] = masked(qlap, h)
            ql[h // 2, second, right] = qh
        wvt[...] = jnp.transpose(wv[...].astype(F32)).astype(BF16)
        for h in range(HEADS):
            vt[h, 2 * HEAD :, :] = jnp.ones((16, 2 * ROWS), BF16)
        top_ref[...] = jnp.full(top_ref.shape, -1e30, F32)
        acc[...] = jnp.zeros(acc.shape, F32)
        sums[...] = jnp.zeros(sums.shape, F32)

    def spin_of(o, side):
        return jnp.transpose(jnp.broadcast_to(g_s[o, side].astype(F32), (ROWS, ROWS)))

    def attend_front(o):
        for n in range(2):
            if n == 0:
                rows = jnp.concatenate([g_lb[o, 0, 0], g_lb[o, 1, 0]], 0)
            else:
                rows = g_t[o].reshape(2 * ROWS, WIDTH)
            keys = dot(rows, wk[...]).astype(BF16)
            for pair in range(2):
                lhs[pair, :, n * ROWS : (n + 1) * ROWS] = keys[:, pair * ROWS : (pair + 1) * ROWS]
            values = dot_t(wvt[...], rows).astype(BF16)
            place = (1 - n) * HEAD
            for h in range(HEADS):
                vt[h, place : place + HEAD, :] = values[h * HEAD : (h + 1) * HEAD]
        for side in range(2):
            rows = slice(side * ROWS, (side + 1) * ROWS)
            s_bias[rows] = g_lb[o, side, 1].astype(F32)
            keys = spin_of(o, side)
            for half in range(2):
                row = g_s[0, (y + half) % 2].astype(F32)
                s_same[rows, half * ROWS : (half + 1) * ROWS] = jnp.where(keys == row, 1.0, 0.0)

    def attend_heads(heads):
        def head_step(h, carry):
            wide = 2 * ROWS
            keys = lhs[h // 2]
            first = dot_t(keys, qa[h, :wide])
            s_score[h % 2] = first + (hg_ref[h] * s_bias[...] + sg_ref[h] * s_same[...])
            old = top_ref[h]
            top = jnp.maximum(old, jnp.max(s_score[h % 2], axis=0, keepdims=True))
            top_ref[h] = top
            shrink = jnp.exp(old - top)
            for n in range(wide // 256):
                part = slice(n * 256, (n + 1) * 256)
                expo = jnp.exp(s_score[h % 2, part] - top)
                s_w[h % 2, part, :wide] = expo.astype(BF16)
                tc = dot_t(lhs[h // 2, part], qa[h, wide:])
                t, c = tc[:, :wide], tc[:, wide:]
                e1 = expo * t
                s_w[h % 2, part, wide : 2 * wide] = e1.astype(BF16)
                s_w[h % 2, part, 2 * wide :] = (e1 * t + expo * c).astype(BF16)
            p = dot(vt[h], s_w[h % 2, :, : 2 * wide])
            r = dot(vt[h, HEAD:, :], s_w[h % 2, :, 2 * wide :])
            a, b = slice(0, 64), slice(64, 128)
            one, two = slice(0, wide), slice(wide, 2 * wide)
            acc[h, 0:64] = acc[h, 0:64] * shrink + p[b, one]
            acc[h, 64:128] = acc[h, 64:128] * shrink + (p[b, two] + p[a, one])
            acc[h, 128:192] = acc[h, 128:192] * shrink + (r[a] + 2.0 * p[a, two])
            sums[h, 0] = sums[h, 0] * shrink + p[128:136, one]
            sums[h, 1] = sums[h, 1] * shrink + p[128:136, two]
            sums[h, 2] = sums[h, 2] * shrink + r[64:72]
            return carry

        for h in heads:
            head_step(h, 0)

    def pass_t(step, side):
        for o in offsets(step):
            if step == 0:
                cross_t.wait_recv()
            else:
                flow(o, side).wait_recv()
            for n in next_of(o, side):
                start(flow(n, side))

    def pass_y(step):
        for o in offsets(step):
            direct_l(o).wait_recv()
            direct_b(o).wait_recv()
            start(cross(o))
            direct_s(o).wait_recv()
            start(cross_s(o))

    def pass_x(step):
        for o in offsets(step):
            cross(o).wait_recv()
            for k in (1, 3, 2):
                start(spread(o, k))

    def pass_core(step):
        for o in offsets(step):
            for k in (1, 3, 2):
                spread(o, k).wait_recv()
            start(mate(o))

    def landed(o):
        cross_s(o).wait_recv()
        mate(o).wait_recv()

    def attend(o, between=()):
        if o == 0:
            cross(0).wait_recv()
            cross_s(0).wait_recv()
            prepare(1)
        elif o != nz // 2:
            landed(o)
        attend_front(o)
        attend_heads((0, 1))
        for call, *args in between:
            call(*args)
        attend_heads((2, 3))

    prepare_own()
    pass_t(0, 1)
    pass_y(1)
    pass_t(1, 0)
    pass_y(2)
    pass_x(1)
    pass_t(1, 1)
    pass_y(3)
    attend(0, ((pass_x, 2), (pass_y, 4), (pass_t, 2, 0)))
    pass_core(1)
    pass_x(3)
    pass_t(2, 1)
    pass_x(4)
    attend(1, ((pass_core, 2), (pass_t, 3, 0)))
    pass_t(3, 1)
    attend(7, ((pass_core, 3),))
    pass_core(4)
    attend(2)
    attend(6)
    attend(3)
    attend(5)
    landed(nz // 2)

    @pl.when(is_own)
    def _():
        copy_x_own.wait()

    @pl.when(not_own)
    def _():
        copy_x.wait()

    lx = g_lb[share_o, share_y, 0, my_half]
    lk = dot(lx, wk[...]).astype(BF16)
    lv = dot_t(wvt[...], lx).astype(BF16)
    lk2 = dot(g_x[...], wk[...]).astype(BF16)
    lv2 = dot_t(wvt[...], g_x[...]).astype(BF16)
    lbias = g_lb[share_o, share_y, 1, my_half, own_lanes].astype(F32)
    s_spin[...] = jnp.where(spin_of(share_o, share_y) == g_s[0, 0].astype(F32), 1.0, 0.0)
    lsame = s_spin[my_half]
    lap_scores = []
    for pair in range(2):
        cols = slice(pair * ROWS, (pair + 1) * ROWS)
        res = dot_t(jnp.concatenate([lk[:, cols], lk2[:, cols]], 1), ql[pair])
        for e in range(2):
            h = pair * 2 + e
            scores = res[:, e * ROWS : (e + 1) * ROWS] + hg_ref[h] * lbias + sg_ref[h] * lsame
            lap_scores.append((scores, res[:, (2 + e) * ROWS : (3 + e) * ROWS]))
    pass_t(4, 0)
    pass_t(4, 1)
    attend(4)


    for h in range(HEADS):
        inv = 1.0 / sums[h, 0, 0:1]
        td = sums[h, 1, 0:1]
        attn = acc[h, 0:64] * inv
        at = (acc[h, 64:128] - attn * td) * inv
        hrows = slice(h * HEAD, (h + 1) * HEAD)
        a_attn[hrows] = attn
        a_tan[hrows] = at
        a_term[hrows] = (acc[h, 128:192] - attn * sums[h, 2, 0:1] - 2.0 * td * at) * inv
    for h in range(HEADS):
        scores, changes = lap_scores[h]
        expo = jnp.exp(scores - top_ref[h, :, own_lanes])
        w = expo.astype(BF16)
        wl = (expo * changes).astype(BF16)
        hrows = slice(h * HEAD, (h + 1) * HEAD)
        lnum = dot(lv[hrows], wl) + dot(lv2[hrows], w)
        lsum = jnp.sum(wl.astype(F32), axis=0, keepdims=True)
        inv = 1.0 / sums[h, 0, 0:1, own_lanes]
        a_term[hrows, own_lanes] += (lnum - a_attn[hrows, own_lanes] * lsum) * inv

    for side in range(2):
        terms = a_term[:, side * ROWS : (side + 1) * ROWS].astype(BF16)
        own[side] = terms.reshape(PEERS // 2, 2 * SHARE, ROWS)

    def rs_copy(k):
        side, inner = group(k)
        return remote(own.at[side, inner], rs.at[k], rs_send.at[k], rs_recv.at[k], group_id(k))

    def high_copy(k):
        return remote(red, high.at[high_y], h_send.at[k], h_recv.at[k], high_id(k))

    def ag_copy(k):
        inner = (member + k) % (PEERS // 2)
        device = {"tan": tan_of(high_y, inner % NX, inner // NX)}
        return remote(ag.at[member], ag.at[member], ag_send.at[k], ag_recv.at[k], device)

    def project_out(value, rows):
        flat = jnp.transpose(value).astype(BF16)
        return dot(flat, wo[...]) + rows.astype(F32)

    loop(1, PEERS, lambda k: rs_copy(k).start())
    other_lanes = pl.ds(pl.multiple_of((1 - y) * ROWS, ROWS), ROWS)
    back_out[...] = project_out(a_tan[:, other_lanes], g_t[0, 1]).astype(BF16)
    copy_back = remote(back_out, back_in, o_send.at[2], o_recv.at[2], other_y)
    copy_back.start()
    rs[0] = own[y, member]
    loop(1, PEERS, lambda k: rs_copy(k).wait_recv())
    red[...] = jnp.sum(rs[...].astype(F32), axis=0).astype(BF16)
    loop(1, highs, lambda k: high_copy(k).start())
    layer_out[...] = project_out(a_attn[:, own_lanes], g_lb[0, 0, 0]).astype(BF16)
    mine = project_out(a_tan[:, own_lanes], g_t[0, 0])
    high[high_y] = red[...]
    loop(1, highs, lambda k: high_copy(k).wait_recv())
    ag[member] = jnp.sum(high[...].astype(F32), axis=0).astype(BF16)
    loop(1, PEERS // 2, lambda k: ag_copy(k).start())
    copy_back.wait_recv()
    theirs = back_in[...].astype(F32)
    tan_out[:, 0] = jnp.where(y == 0, mine, theirs).astype(BF16)
    tan_out[:, 1] = jnp.where(y == 0, theirs, mine).astype(BF16)
    for copy in started:
        copy.wait_send()
    copy_back.wait_send()
    loop(1, PEERS, lambda k: rs_copy(k).wait_send())
    loop(1, highs, lambda k: high_copy(k).wait_send())
    loop(1, PEERS // 2, lambda k: ag_copy(k).wait_recv())
    lap_out[...] = project_out(ag[...].reshape(WIDTH, ROWS).astype(F32), lap_own[...])
    loop(1, PEERS // 2, lambda k: ag_copy(k).wait_send())


def solution(mesh):
    blks, tans = mesh.shape["blk"], mesh.shape["tan"]
    nz = blks // 2

    def on_device(layer, lap, tangent, spin, bias, wq, wk, wv, wo, hg, sg):
        spins = spin.reshape(1, ROWS)
        any_spec = pl.BlockSpec(memory_space=pl.ANY)
        smem = pl.BlockSpec(memory_space=pltpu.SMEM)
        vmem = pl.BlockSpec(memory_space=pltpu.VMEM)
        sq = (WIDTH, WIDTH)
        scratch = [
            pltpu.VMEM(sq, BF16),
            pltpu.VMEM(sq, BF16),
            pltpu.VMEM(sq, BF16),
            pltpu.VMEM(sq, BF16),
            pltpu.VMEM(sq, BF16),
            pltpu.VMEM((ROWS, WIDTH), BF16),
            pltpu.VMEM((ROWS, WIDTH), BF16),
            pltpu.VMEM((ROWS, 2, WIDTH), BF16),
            pltpu.VMEM((nz, 2, 2, ROWS, WIDTH), BF16),
            pltpu.VMEM((nz, 2, ROWS, WIDTH), BF16),
            pltpu.VMEM((nz, 2, 1, ROWS), jnp.int32),
            pltpu.VMEM((HALF, WIDTH), BF16),
            pltpu.VMEM((HEADS, 6 * ROWS, WIDTH), BF16),
            pltpu.VMEM((2, 4 * ROWS, WIDTH), BF16),
            pltpu.VMEM((2, 2 * ROWS, WIDTH), BF16),
            pltpu.VMEM((HEADS, 2 * HEAD + 16, 2 * ROWS), BF16),
            pltpu.VMEM((2 * ROWS, 2 * ROWS), F32),
            pltpu.VMEM((2, 2 * ROWS, 2 * ROWS), F32),
            pltpu.VMEM((2, 2 * ROWS, 6 * ROWS), BF16),
            pltpu.VMEM((2 * ROWS, 2 * ROWS), F32),
            pltpu.VMEM((ROWS, ROWS), F32),
            pltpu.VMEM((HEADS, 1, 2 * ROWS), F32),
            pltpu.VMEM((HEADS, 3 * HEAD, 2 * ROWS), F32),
            pltpu.VMEM((HEADS, 3, 8, 2 * ROWS), F32),
            pltpu.VMEM((WIDTH, 2 * ROWS), F32),
            pltpu.VMEM((WIDTH, 2 * ROWS), F32),
            pltpu.VMEM((WIDTH, 2 * ROWS), F32),
            pltpu.VMEM((2, PEERS // 2, 2 * SHARE, ROWS), BF16),
            pltpu.VMEM((PEERS, 2 * SHARE, ROWS), BF16),
            pltpu.VMEM((2 * SHARE, ROWS), BF16),
            pltpu.VMEM((tans // (2 * NX), 2 * SHARE, ROWS), BF16),
            pltpu.VMEM((PEERS // 2, 2 * SHARE, ROWS), BF16),
            pltpu.VMEM((ROWS, WIDTH), BF16),
            pltpu.VMEM((ROWS, WIDTH), BF16),
            pltpu.SemaphoreType.DMA((11,)),
        ]
        one, two = (nz,), (nz, 2)
        shapes = (one, one, one, one, one, (nz, NX), one, two, (3,))
        for shape in shapes + ((PEERS,), (tans // (2 * NX),), (PEERS // 2,)):
            scratch += [pltpu.SemaphoreType.DMA(shape)] * 2
        layer_out, tan_out, lap_out = pl.pallas_call(
            functools.partial(kernel, nz, tans),
            out_shape=(
                jax.ShapeDtypeStruct((ROWS, WIDTH), BF16),
                jax.ShapeDtypeStruct((ROWS, 2, WIDTH), BF16),
                jax.ShapeDtypeStruct((ROWS, WIDTH), F32),
            ),
            in_specs=[any_spec] * 9 + [smem, smem],
            out_specs=(vmem, vmem, vmem),
            scratch_shapes=scratch,
            compiler_params=pltpu.CompilerParams(collective_id=0, has_side_effects=True),
            name="laplacian_attention",
        )(layer, lap, tangent, spins, bias, wq, wk, wv, wo, hg, sg)
        return layer_out, tan_out, lap_out

    in_specs = (
        P("blk", None),
        P("blk", None),
        P("blk", "tan", None),
        P("blk"),
        P("blk", None),
        P(),
        P(),
        P(),
        P(),
        P(),
        P(),
    )
    out_specs = (P("blk", None), P("blk", "tan", None), P("blk", None))
    return jax.shard_map(
        on_device, mesh=mesh, in_specs=in_specs, out_specs=out_specs, check_vma=False
    )
```

```python
import functools

import jax
import jax.numpy as jnp
from jax import lax
from jax.experimental import pallas as pl
from jax.experimental.pallas import tpu as pltpu
from jax.sharding import PartitionSpec as P

MESH = pl.DeviceIdType.MESH
F32 = jnp.float32
BF16 = jnp.bfloat16
ROWS = 128
HALF = 64
SHARE = 16
WIDTH = 256
HEADS = 4
HEAD = 64
NX = 4
PEERS = 16


def dot(a, b):
    return jnp.dot(a, b, preferred_element_type=F32)


def dot_t(a, b):
    return lax.dot_general(a, b, (((1,), (1,)), ((), ())), preferred_element_type=F32)


def kernel(
    nz,
    tans,
    layer_hbm,
    lap_hbm,
    tan_hbm,
    spin_hbm,
    bias_hbm,
    wq_hbm,
    wk_hbm,
    wv_hbm,
    wo_hbm,
    hg_ref,
    sg_ref,
    layer_out,
    tan_out,
    lap_out,
    wq,
    wk,
    wv,
    wo,
    wvt,
    lap_own,
    tan_own,
    tan_raw,
    g_lb,
    g_t,
    g_s,
    g_x,
    qa,
    ql,
    lhs,
    vt,
    s_bias,
    s_score,
    s_w,
    s_same,
    s_spin,
    top_ref,
    acc,
    sums,
    a_attn,
    a_tan,
    a_term,
    own,
    rs,
    red,
    high,
    ag,
    back_out,
    back_in,
    local_sem,
    d_l_send,
    d_l_recv,
    d_b_send,
    d_b_recv,
    d_s_send,
    d_s_recv,
    y_send,
    y_recv,
    ys_send,
    ys_recv,
    x_send,
    x_recv,
    c_send,
    c_recv,
    t_send,
    t_recv,
    o_send,
    o_recv,
    rs_send,
    rs_recv,
    h_send,
    h_recv,
    ag_send,
    ag_recv,
):
    blk = lax.axis_index("blk")
    tan = lax.axis_index("tan")
    z = blk // 2
    y = blk % 2
    core = tan % 2
    x = (tan // 2) % NX
    high_y = tan // (2 * NX)
    highs = tans // (2 * NX)
    member = core * NX + x
    me = y * (PEERS // 2) + member
    share = pl.ds(pl.multiple_of(member * SHARE, SHARE), SHARE)
    my_half = pl.ds(pl.multiple_of(core * HALF, HALF), HALF)
    own_lanes = pl.ds(pl.multiple_of(y * ROWS, ROWS), ROWS)

    def tan_of(high_at, x_at, core_at):
        return (high_at * NX + x_at) * 2 + core_at

    def group(k):
        at = (me + k) % PEERS
        inner = at % (PEERS // 2)
        return at // (PEERS // 2), inner

    def group_id(k):
        side, inner = group(k)
        return {"blk": z * 2 + side, "tan": tan_of(high_y, inner % NX, inner // NX)}

    def z_id(k):
        return {"blk": ((z + k) % nz) * 2 + y}

    def high_id(k):
        return {"tan": tan_of((high_y + k) % highs, x, core)}

    share_o = tan // 4
    share_y = (tan // 2) % 2
    is_own = tan < 2
    not_own = jnp.logical_not(is_own)
    share_to = ((z + share_o) % nz) * 2 + (y + share_y) % 2
    share_from = ((z + nz - share_o) % nz) * 2 + (y + share_y) % 2

    barrier = pltpu.get_barrier_semaphore()

    def loop(first, last, body):
        def run(k, carry):
            body(k)
            return carry

        lax.fori_loop(first, last, run, 0)

    def greet(device):
        pl.semaphore_signal(barrier, inc=1, device_id=device, device_id_type=MESH)

    loop(1, nz, lambda k: greet(z_id(k)))
    loop(1, PEERS, lambda k: greet(group_id(k)))
    loop(1, highs, lambda k: greet(high_id(k)))

    @pl.when(not_own)
    def _():
        greet({"blk": share_from})

    pair_cols = pl.ds(pl.multiple_of(z * 2 * ROWS, 2 * ROWS), 2 * ROWS)
    local = [
        (tan_hbm, tan_raw),
        (layer_hbm, g_lb.at[0, 0, 0]),
        (bias_hbm.at[:, pair_cols], g_lb.at[0, 0, 1]),
        (spin_hbm, g_s.at[0, 0]),
        (wq_hbm, wq),
        (wk_hbm, wk),
        (wv_hbm, wv),
        (lap_hbm, lap_own),
        (wo_hbm, wo),
    ]
    local = [
        pltpu.make_async_copy(src, dst, local_sem.at[n]) for n, (src, dst) in enumerate(local)
    ]
    for copy in local:
        copy.start()

    other_y = {"blk": z * 2 + (1 - y)}
    other_core = {"tan": tan + 1 - 2 * core}
    started = []

    def remote(src, dst, send, recv, device):
        return pltpu.make_async_remote_copy(
            src_ref=src,
            dst_ref=dst,
            send_sem=send,
            recv_sem=recv,
            device_id=device,
            device_id_type=MESH,
        )

    def start(copy):
        copy.start()
        started.append(copy)

    def direct_l(o):
        there = z_id(o)
        return remote(
            layer_hbm.at[share], g_lb.at[o, 0, 0, share], d_l_send.at[o], d_l_recv.at[o], there
        )

    def direct_b(o):
        there = (z + o) % nz
        columns = pl.ds(pl.multiple_of(there * 2 * ROWS, 2 * ROWS), 2 * ROWS)
        return remote(
            bias_hbm.at[share, columns],
            g_lb.at[o, 0, 1, share],
            d_b_send.at[o],
            d_b_recv.at[o],
            z_id(o),
        )

    def direct_s(o):
        return remote(spin_hbm, g_s.at[o, 0], d_s_send.at[o], d_s_recv.at[o], z_id(o))

    def cross(o):
        if o == 0:
            return remote(g_lb.at[0, 0], g_lb.at[0, 1], y_send.at[0], y_recv.at[0], other_y)
        return remote(
            g_lb.at[o, 0, :, share],
            g_lb.at[o, 1, :, share],
            y_send.at[o],
            y_recv.at[o],
            other_y,
        )

    def cross_s(o):
        return remote(g_s.at[o, 0], g_s.at[o, 1], ys_send.at[o], ys_recv.at[o], other_y)

    def spread(o, side, k):
        piece = g_lb.at[o, side, :, share]
        device = {"tan": tan_of(high_y, (x + k) % NX, core)}
        return remote(piece, piece, x_send.at[o, side, k], x_recv.at[o, side, k], device)

    def mate(o):
        piece = g_lb.at[o, :, :, my_half]
        return remote(piece, piece, c_send.at[o], c_recv.at[o], other_core)

    cross_t = remote(tan_own, g_t.at[0, 1], o_send.at[0], o_recv.at[0], other_y)

    def last_up(side):
        return nz // 2 if side == 0 else nz - 1 - nz // 2

    def flow(o, side):
        if o <= last_up(side):
            src, device = o - 1, z_id(1)
        else:
            src, device = (o + 1) % nz, z_id(nz - 1)
        return remote(
            g_t.at[src, side], g_t.at[o, side], t_send.at[o, side], t_recv.at[o, side], device
        )

    def next_of(o, side):
        last = last_up(side)
        if o == 0:
            return [n for n in sorted({1, nz - 1}) if n <= 1 or n > last]
        if o <= last:
            return [o + 1] if o < last else []
        return [o - 1] if o - 1 > last else []

    def offsets(step):
        return sorted({step, (nz - step) % nz})

    copy_x = remote(lap_hbm.at[my_half], g_x, o_send.at[1], o_recv.at[1], {"blk": share_to})
    copy_x_own = pltpu.make_async_copy(lap_hbm.at[my_half], g_x, local_sem.at[9])

    for copy in local[:4]:
        copy.wait()
    raw = tan_raw[...].astype(F32)
    first, second = raw[:, 0].astype(BF16), raw[:, 1].astype(BF16)
    g_t[0, 0] = jnp.where(y == 0, first, second)
    tan_own[...] = jnp.where(y == 0, second, first)
    greeted = nz - 1 + PEERS - 1 + highs - 1
    pl.semaphore_wait(barrier, greeted + jnp.where(is_own, 0, 1))

    steps = nz // 2
    start(cross_t)
    start(cross(0))
    start(cross_s(0))
    for step in range(1, steps + 1):
        for o in offsets(step):
            start(direct_l(o))
            start(direct_b(o))
            start(direct_s(o))
        if step == 1:
            for o in next_of(0, 0):
                start(flow(o, 0))

    @pl.when(is_own)
    def _():
        copy_x_own.start()

    @pl.when(not_own)
    def _():
        copy_x.start()

    for copy in local[4:]:
        copy.wait()

    lanes = lax.broadcasted_iota(jnp.int32, (ROWS, ROWS), 1)
    left, right = slice(0, ROWS), slice(ROWS, 2 * ROWS)

    def queries(rows):
        return dot(rows, wq[...]).astype(BF16).astype(F32) * 0.125

    def masked(value, h, scale=1.0):
        pair, e = h // 2, h % 2
        keep = (lanes >= e * HEAD) & (lanes < (e + 1) * HEAD)
        return jnp.where(keep, value[:, pair * ROWS : (pair + 1) * ROWS] * scale, 0.0).astype(BF16)

    zero = jnp.zeros((ROWS, ROWS), BF16)

    def prepare(side):
        at = (y + side) % 2
        q = queries(g_lb[0, side, 0])
        qt = queries(g_t[0, side])

        def rows(n):
            return pl.ds(pl.multiple_of(n * 2 * ROWS + at * ROWS, ROWS), ROWS)

        for h in range(HEADS):
            qh = masked(q, h)
            qa[h, rows(0), left] = qh
            qa[h, rows(0), right] = zero
            qa[h, rows(1), left] = masked(qt, h)
            qa[h, rows(1), right] = qh
            qa[h, rows(2), left] = zero
            qa[h, rows(2), right] = masked(qt, h, 2.0)
        return q

    def prepare_own():
        q = prepare(0)
        qlap = queries(lap_own[...])
        for h in range(HEADS):
            first = slice((h % 2) * ROWS, (h % 2 + 1) * ROWS)
            second = slice((2 + h % 2) * ROWS, (3 + h % 2) * ROWS)
            qh = masked(q, h)
            ql[h // 2, first, left] = qh
            ql[h // 2, first, right] = zero
            ql[h // 2, second, left] = masked(qlap, h)
            ql[h // 2, second, right] = qh
        wvt[...] = jnp.transpose(wv[...].astype(F32)).astype(BF16)
        for h in range(HEADS):
            vt[h, 2 * HEAD :, :] = jnp.ones((16, 2 * ROWS), BF16)
        top_ref[...] = jnp.full(top_ref.shape, -1e30, F32)
        acc[...] = jnp.zeros(acc.shape, F32)
        sums[...] = jnp.zeros(sums.shape, F32)

    def spin_of(o, side):
        return jnp.transpose(jnp.broadcast_to(g_s[o, side].astype(F32), (ROWS, ROWS)))

    def attend_front(o):
        for n in range(2):
            if n == 0:
                rows = jnp.concatenate([g_lb[o, 0, 0], g_lb[o, 1, 0]], 0)
            else:
                rows = g_t[o].reshape(2 * ROWS, WIDTH)
            keys = dot(rows, wk[...]).astype(BF16)
            for pair in range(2):
                lhs[pair, :, n * ROWS : (n + 1) * ROWS] = keys[:, pair * ROWS : (pair + 1) * ROWS]
            values = dot_t(wvt[...], rows).astype(BF16)
            place = (1 - n) * HEAD
            for h in range(HEADS):
                vt[h, place : place + HEAD, :] = values[h * HEAD : (h + 1) * HEAD]
        for side in range(2):
            rows = slice(side * ROWS, (side + 1) * ROWS)
            s_bias[rows] = g_lb[o, side, 1].astype(F32)
            keys = spin_of(o, side)
            for half in range(2):
                row = g_s[0, (y + half) % 2].astype(F32)
                s_same[rows, half * ROWS : (half + 1) * ROWS] = jnp.where(keys == row, 1.0, 0.0)

    def attend_heads(heads):
        def head_step(h, carry):
            wide = 2 * ROWS
            keys = lhs[h // 2]
            first = dot_t(keys, qa[h, :wide])
            s_score[h % 2] = first + (hg_ref[h] * s_bias[...] + sg_ref[h] * s_same[...])
            old = top_ref[h]
            top = jnp.maximum(old, jnp.max(s_score[h % 2], axis=0, keepdims=True))
            top_ref[h] = top
            shrink = jnp.exp(old - top)
            for n in range(wide // 256):
                part = slice(n * 256, (n + 1) * 256)
                expo = jnp.exp(s_score[h % 2, part] - top)
                s_w[h % 2, part, :wide] = expo.astype(BF16)
                tc = dot_t(lhs[h // 2, part], qa[h, wide:])
                t, c = tc[:, :wide], tc[:, wide:]
                e1 = expo * t
                s_w[h % 2, part, wide : 2 * wide] = e1.astype(BF16)
                s_w[h % 2, part, 2 * wide :] = (e1 * t + expo * c).astype(BF16)
            p = dot(vt[h], s_w[h % 2, :, : 2 * wide])
            r = dot(vt[h, HEAD:, :], s_w[h % 2, :, 2 * wide :])
            a, b = slice(0, 64), slice(64, 128)
            one, two = slice(0, wide), slice(wide, 2 * wide)
            acc[h, 0:64] = acc[h, 0:64] * shrink + p[b, one]
            acc[h, 64:128] = acc[h, 64:128] * shrink + (p[b, two] + p[a, one])
            acc[h, 128:192] = acc[h, 128:192] * shrink + (r[a] + 2.0 * p[a, two])
            sums[h, 0] = sums[h, 0] * shrink + p[128:136, one]
            sums[h, 1] = sums[h, 1] * shrink + p[128:136, two]
            sums[h, 2] = sums[h, 2] * shrink + r[64:72]
            return carry

        for h in heads:
            head_step(h, 0)

    def pass_t(step, side):
        for o in offsets(step):
            if step == 0:
                cross_t.wait_recv()
            else:
                flow(o, side).wait_recv()
            for n in next_of(o, side):
                start(flow(n, side))

    def pass_y(step):
        for o in offsets(step):
            direct_l(o).wait_recv()
            direct_b(o).wait_recv()
            start(cross(o))
            for k in (1, 3, 2):
                start(spread(o, 0, k))
            direct_s(o).wait_recv()
            start(cross_s(o))

    def pass_x(step):
        for o in offsets(step):
            cross(o).wait_recv()
            for k in (1, 3, 2):
                start(spread(o, 1, k))

    def pass_core(step):
        for o in offsets(step):
            for side in range(2):
                for k in (1, 3, 2):
                    spread(o, side, k).wait_recv()
            start(mate(o))

    def landed(o):
        cross_s(o).wait_recv()
        mate(o).wait_recv()

    def attend(o, between=()):
        if o == 0:
            cross(0).wait_recv()
            cross_s(0).wait_recv()
            prepare(1)
        elif o != nz // 2:
            landed(o)
        attend_front(o)
        attend_heads((0, 1))
        for call, *args in between:
            call(*args)
        attend_heads((2, 3))

    prepare_own()
    pass_t(0, 1)
    pass_y(1)
    pass_t(1, 0)
    pass_y(2)
    pass_x(1)
    pass_t(1, 1)
    pass_y(3)
    attend(0, ((pass_x, 2), (pass_y, 4), (pass_t, 2, 0)))
    pass_core(1)
    pass_x(3)
    pass_t(2, 1)
    pass_x(4)
    attend(1, ((pass_core, 2),))
    attend(7, ((pass_core, 3),))
    attend(2, ((pass_t, 3, 0),))
    attend(6, ((pass_t, 3, 1), (pass_core, 4)))
    attend(3)
    attend(5)
    landed(nz // 2)

    @pl.when(is_own)
    def _():
        copy_x_own.wait()

    @pl.when(not_own)
    def _():
        copy_x.wait()

    lx = g_lb[share_o, share_y, 0, my_half]
    lk = dot(lx, wk[...]).astype(BF16)
    lv = dot_t(wvt[...], lx).astype(BF16)
    lk2 = dot(g_x[...], wk[...]).astype(BF16)
    lv2 = dot_t(wvt[...], g_x[...]).astype(BF16)
    lbias = g_lb[share_o, share_y, 1, my_half, own_lanes].astype(F32)
    s_spin[...] = jnp.where(spin_of(share_o, share_y) == g_s[0, 0].astype(F32), 1.0, 0.0)
    lsame = s_spin[my_half]
    lap_scores = []
    for pair in range(2):
        cols = slice(pair * ROWS, (pair + 1) * ROWS)
        res = dot_t(jnp.concatenate([lk[:, cols], lk2[:, cols]], 1), ql[pair])
        for e in range(2):
            h = pair * 2 + e
            scores = res[:, e * ROWS : (e + 1) * ROWS] + hg_ref[h] * lbias + sg_ref[h] * lsame
            lap_scores.append((scores, res[:, (2 + e) * ROWS : (3 + e) * ROWS]))
    pass_t(4, 0)
    pass_t(4, 1)
    attend(4)


    for h in range(HEADS):
        inv = 1.0 / sums[h, 0, 0:1]
        td = sums[h, 1, 0:1]
        attn = acc[h, 0:64] * inv
        at = (acc[h, 64:128] - attn * td) * inv
        hrows = slice(h * HEAD, (h + 1) * HEAD)
        a_attn[hrows] = attn
        a_tan[hrows] = at
        a_term[hrows] = (acc[h, 128:192] - attn * sums[h, 2, 0:1] - 2.0 * td * at) * inv
    for h in range(HEADS):
        scores, changes = lap_scores[h]
        expo = jnp.exp(scores - top_ref[h, :, own_lanes])
        w = expo.astype(BF16)
        wl = (expo * changes).astype(BF16)
        hrows = slice(h * HEAD, (h + 1) * HEAD)
        lnum = dot(lv[hrows], wl) + dot(lv2[hrows], w)
        lsum = jnp.sum(wl.astype(F32), axis=0, keepdims=True)
        inv = 1.0 / sums[h, 0, 0:1, own_lanes]
        a_term[hrows, own_lanes] += (lnum - a_attn[hrows, own_lanes] * lsum) * inv

    for side in range(2):
        terms = a_term[:, side * ROWS : (side + 1) * ROWS].astype(BF16)
        own[side] = terms.reshape(PEERS // 2, 2 * SHARE, ROWS)

    def rs_copy(k):
        side, inner = group(k)
        return remote(own.at[side, inner], rs.at[k], rs_send.at[k], rs_recv.at[k], group_id(k))

    def high_copy(k):
        return remote(red, high.at[high_y], h_send.at[k], h_recv.at[k], high_id(k))

    def ag_copy(k):
        inner = (member + k) % (PEERS // 2)
        device = {"tan": tan_of(high_y, inner % NX, inner // NX)}
        return remote(ag.at[member], ag.at[member], ag_send.at[k], ag_recv.at[k], device)

    def project_out(value, rows):
        flat = jnp.transpose(value).astype(BF16)
        return dot(flat, wo[...]) + rows.astype(F32)

    loop(1, PEERS, lambda k: rs_copy(k).start())
    other_lanes = pl.ds(pl.multiple_of((1 - y) * ROWS, ROWS), ROWS)
    back_out[...] = project_out(a_tan[:, other_lanes], g_t[0, 1]).astype(BF16)
    copy_back = remote(back_out, back_in, o_send.at[2], o_recv.at[2], other_y)
    copy_back.start()
    rs[0] = own[y, member]
    loop(1, PEERS, lambda k: rs_copy(k).wait_recv())
    red[...] = jnp.sum(rs[...].astype(F32), axis=0).astype(BF16)
    loop(1, highs, lambda k: high_copy(k).start())
    layer_out[...] = project_out(a_attn[:, own_lanes], g_lb[0, 0, 0]).astype(BF16)
    mine = project_out(a_tan[:, own_lanes], g_t[0, 0])
    high[high_y] = red[...]
    loop(1, highs, lambda k: high_copy(k).wait_recv())
    ag[member] = jnp.sum(high[...].astype(F32), axis=0).astype(BF16)
    loop(1, PEERS // 2, lambda k: ag_copy(k).start())
    copy_back.wait_recv()
    theirs = back_in[...].astype(F32)
    tan_out[:, 0] = jnp.where(y == 0, mine, theirs).astype(BF16)
    tan_out[:, 1] = jnp.where(y == 0, theirs, mine).astype(BF16)
    for copy in started:
        copy.wait_send()
    copy_back.wait_send()
    loop(1, PEERS, lambda k: rs_copy(k).wait_send())
    loop(1, highs, lambda k: high_copy(k).wait_send())
    loop(1, PEERS // 2, lambda k: ag_copy(k).wait_recv())
    lap_out[...] = project_out(ag[...].reshape(WIDTH, ROWS).astype(F32), lap_own[...])
    loop(1, PEERS // 2, lambda k: ag_copy(k).wait_send())


def solution(mesh):
    blks, tans = mesh.shape["blk"], mesh.shape["tan"]
    nz = blks // 2

    def on_device(layer, lap, tangent, spin, bias, wq, wk, wv, wo, hg, sg):
        spins = spin.reshape(1, ROWS)
        any_spec = pl.BlockSpec(memory_space=pl.ANY)
        smem = pl.BlockSpec(memory_space=pltpu.SMEM)
        vmem = pl.BlockSpec(memory_space=pltpu.VMEM)
        sq = (WIDTH, WIDTH)
        scratch = [
            pltpu.VMEM(sq, BF16),
            pltpu.VMEM(sq, BF16),
            pltpu.VMEM(sq, BF16),
            pltpu.VMEM(sq, BF16),
            pltpu.VMEM(sq, BF16),
            pltpu.VMEM((ROWS, WIDTH), BF16),
            pltpu.VMEM((ROWS, WIDTH), BF16),
            pltpu.VMEM((ROWS, 2, WIDTH), BF16),
            pltpu.VMEM((nz, 2, 2, ROWS, WIDTH), BF16),
            pltpu.VMEM((nz, 2, ROWS, WIDTH), BF16),
            pltpu.VMEM((nz, 2, 1, ROWS), jnp.int32),
            pltpu.VMEM((HALF, WIDTH), BF16),
            pltpu.VMEM((HEADS, 6 * ROWS, WIDTH), BF16),
            pltpu.VMEM((2, 4 * ROWS, WIDTH), BF16),
            pltpu.VMEM((2, 2 * ROWS, WIDTH), BF16),
            pltpu.VMEM((HEADS, 2 * HEAD + 16, 2 * ROWS), BF16),
            pltpu.VMEM((2 * ROWS, 2 * ROWS), F32),
            pltpu.VMEM((2, 2 * ROWS, 2 * ROWS), F32),
            pltpu.VMEM((2, 2 * ROWS, 6 * ROWS), BF16),
            pltpu.VMEM((2 * ROWS, 2 * ROWS), F32),
            pltpu.VMEM((ROWS, ROWS), F32),
            pltpu.VMEM((HEADS, 1, 2 * ROWS), F32),
            pltpu.VMEM((HEADS, 3 * HEAD, 2 * ROWS), F32),
            pltpu.VMEM((HEADS, 3, 8, 2 * ROWS), F32),
            pltpu.VMEM((WIDTH, 2 * ROWS), F32),
            pltpu.VMEM((WIDTH, 2 * ROWS), F32),
            pltpu.VMEM((WIDTH, 2 * ROWS), F32),
            pltpu.VMEM((2, PEERS // 2, 2 * SHARE, ROWS), BF16),
            pltpu.VMEM((PEERS, 2 * SHARE, ROWS), BF16),
            pltpu.VMEM((2 * SHARE, ROWS), BF16),
            pltpu.VMEM((tans // (2 * NX), 2 * SHARE, ROWS), BF16),
            pltpu.VMEM((PEERS // 2, 2 * SHARE, ROWS), BF16),
            pltpu.VMEM((ROWS, WIDTH), BF16),
            pltpu.VMEM((ROWS, WIDTH), BF16),
            pltpu.SemaphoreType.DMA((11,)),
        ]
        one, two = (nz,), (nz, 2)
        shapes = (one, one, one, one, one, (nz, 2, NX), one, two, (3,))
        for shape in shapes + ((PEERS,), (tans // (2 * NX),), (PEERS // 2,)):
            scratch += [pltpu.SemaphoreType.DMA(shape)] * 2
        layer_out, tan_out, lap_out = pl.pallas_call(
            functools.partial(kernel, nz, tans),
            out_shape=(
                jax.ShapeDtypeStruct((ROWS, WIDTH), BF16),
                jax.ShapeDtypeStruct((ROWS, 2, WIDTH), BF16),
                jax.ShapeDtypeStruct((ROWS, WIDTH), F32),
            ),
            in_specs=[any_spec] * 9 + [smem, smem],
            out_specs=(vmem, vmem, vmem),
            scratch_shapes=scratch,
            compiler_params=pltpu.CompilerParams(collective_id=0, has_side_effects=True),
            name="laplacian_attention",
        )(layer, lap, tangent, spins, bias, wq, wk, wv, wo, hg, sg)
        return layer_out, tan_out, lap_out

    in_specs = (
        P("blk", None),
        P("blk", None),
        P("blk", "tan", None),
        P("blk"),
        P("blk", None),
        P(),
        P(),
        P(),
        P(),
        P(),
        P(),
    )
    out_specs = (P("blk", None), P("blk", "tan", None), P("blk", None))
    return jax.shard_map(
        on_device, mesh=mesh, in_specs=in_specs, out_specs=out_specs, check_vma=False
    )
```
